512 devices in a mesh: row: 16 (over y, core), col: 32 (over z, x).
Axes of the slice: x: 4, y: 8, z: 8, core: 2. Of those that a mesh axis runs over, the one named last changes fastest.
Arguments:
- points: bfloat16 [128, 65536], P(None, ('row', 'col')), may hold values from -6 to 6
- inv_scale: float32 [128], replicated, may hold values from 0.07 to 0.22
- basis: bfloat16 [65536, 4096], P(('row', 'col')), may hold values from -0.25 to 0.25
- shrink: float32 [4096], replicated, may hold values from 0.02 to 1
- solution: float32 [33, 65536], P(None, ('row', 'col')), may hold values from -6 to 6
- residual: float32 [33, 65536], P(None, ('row', 'col')), may hold values from -6 to 6
- direction_prev: float32 [33, 65536], P(None, ('row', 'col')), may hold values from -6 to 6
- rz_prev: float32 [33], replicated, may hold values from 65536 to 262144
Outputs:
- solution_next: float32 [33, 65536], P(None, ('row', 'col'))
- residual_next: float32 [33, 65536], P(None, ('row', 'col'))
- direction: float32 [33, 65536], P(None, ('row', 'col'))
The draws below stay inside these ranges and needn't reach their ends.
All inputs are finite; a program needn't handle non-finite values.
Results may differ from the reference program's by a relative error of at most 0.019.
Values may be sent and summed in bfloat16 or wider, within the bound.
A program may use at most 64 MiB of HBM per device.

```python
import math
import jax
import jax.numpy as jnp
from jax import lax

FEAT = 128
RANK = 4096
RHS = 33
N_PTS = 65536


def with_spikes(entries, own_key, source, target, shards_of, factor):
    def block_of(position):
        return (jnp.arange(entries.shape[position]) // (entries.shape[position] // shards_of)).reshape((-1,) + (1,) * (entries.ndim - 1 - position))

    first = jax.random.permutation(own_key, shards_of)[block_of(target)]
    other_side = (block_of(target) + shards_of // 2) % shards_of
    return jnp.where((block_of(source) == first) | (block_of(source) == other_side), factor * entries, entries)


def block_scale(own_key, extent, cuts, least, top_value):
    def one(dim, shards_of):
        heights = jax.random.uniform(jax.random.fold_in(jax.random.fold_in(own_key, 6), dim), (shards_of,), jnp.float32, least / len(cuts), top_value / len(cuts))
        return jnp.repeat(jnp.exp(heights), extent[dim] // shards_of).reshape((-1,) + (1,) * (len(extent) - dim - 1))

    gain = one(*cuts[0])
    for cut in cuts[1:]:
        gain = gain * one(*cut)
    return gain


def normal_values(key, extent, spread, bound, shards=(), held_as=jnp.bfloat16):
    factor_of = block_scale(key, extent, shards, -0.22, 0.18) if shards else 1.0
    values = jax.random.normal(key, extent, jnp.float32) * spread * factor_of
    return jnp.minimum(jnp.maximum(values, -bound), bound).astype(held_as)


def noise_with(stream_key, shape, spread, limit, pieces, heavy, kind=jnp.bfloat16):
    drawn = spread * jax.random.normal(stream_key, shape, jnp.float32)
    if pieces:
        drawn = drawn * block_scale(stream_key, shape, pieces, -0.22, 0.18)
    return jnp.clip(with_spikes(drawn, jax.random.fold_in(stream_key, 3), *heavy), -limit, limit).astype(kind)


def setup_inputs(seed: int = 0) -> dict:
    key_of = jax.random.split(jax.random.key(seed), 9)
    points = normal_values(key_of[0], (FEAT, N_PTS), 1.0, 6.0, ((1, 512),))
    inv_scale = jnp.clip(jnp.exp(jax.random.uniform(key_of[1], (FEAT,), jnp.float32, math.log(0.07), math.log(0.22))), 0.07, 0.22)
    basis = noise_with(key_of[2], (N_PTS, RANK), (N_PTS // 8) ** -0.5, 0.25, ((0, 512),), (0, 1, 512, 6.0))
    shrink = jnp.clip(jnp.exp(jax.random.uniform(key_of[3], (RANK,), jnp.float32, math.log(0.02), math.log(1.0))), 0.02, 1.0)
    solution = normal_values(key_of[4], (RHS, N_PTS), 1.0, 6.0, ((1, 512),), jnp.float32)
    residual = normal_values(key_of[5], (RHS, N_PTS), 1.0, 6.0, ((1, 512),), jnp.float32)
    direction_prev = normal_values(key_of[6], (RHS, N_PTS), 1.0, 6.0, ((1, 512),), jnp.float32)
    rz_prev = jnp.clip(jnp.exp(jax.random.uniform(key_of[7], (RHS,), jnp.float32, math.log(65536.0), math.log(262144.0))), 65536.0, 262144.0)
    return {"points": points, "inv_scale": inv_scale, "basis": basis, "shrink": shrink, "solution": solution, "residual": residual, "direction_prev": direction_prev, "rz_prev": rz_prev}


noise_level = 0.25


def reference(points, inv_scale, basis, shrink, solution, residual, direction_prev, rz_prev):
    scaled = (points * inv_scale[:, None]).astype(jnp.bfloat16)
    residual_bf = residual.astype(jnp.bfloat16)
    projected = jnp.dot(residual_bf, basis, preferred_element_type=jnp.float32)
    correction = ((shrink - 1.0)[None, :] * projected).astype(jnp.bfloat16)
    precond = residual + jnp.dot(correction, basis.T, preferred_element_type=jnp.float32)
    precond_inner = jnp.sum(residual * precond, axis=1)
    direction = precond + (precond_inner / rz_prev)[:, None] * direction_prev
    direction_bf = direction.astype(jnp.bfloat16)
    squares = jnp.sum(jnp.square(scaled.astype(jnp.float32)), axis=0)
    width = min(1024, N_PTS)
    count = N_PTS // width

    def one_block(offset):
        rows = lax.dynamic_slice_in_dim(scaled, offset * width, width, 1)
        row_sq = lax.dynamic_slice_in_dim(squares, offset * width, width, 0)
        cross = jnp.dot(scaled.T, rows, preferred_element_type=jnp.float32)
        distance = jnp.maximum(squares[:, None] + row_sq[None, :] - 2.0 * cross, 0.0)
        tile = jnp.exp(-0.5 * distance).astype(jnp.bfloat16)
        return jnp.dot(direction_bf, tile, preferred_element_type=jnp.float32)

    blocks = lax.map(one_block, jnp.arange(count, dtype=jnp.int32))
    image = jnp.transpose(blocks, (1, 0, 2)).reshape(RHS, N_PTS) + noise_level * direction
    curvature = jnp.sum(direction * image, axis=1)
    alpha = precond_inner / curvature
    solution_next = solution + alpha[:, None] * direction
    residual_next = residual - alpha[:, None] * image
    return solution_next, residual_next, direction
```

```python
import functools

import jax
import jax.numpy as jnp
from jax import lax
from jax.experimental import pallas as pl
from jax.experimental.pallas import tpu as pltpu
from jax.sharding import PartitionSpec as P

MESH = pl.DeviceIdType.MESH
BF = jnp.bfloat16
F32 = jnp.float32
NOISE = 0.25
G = 16
L = 128
HALF = G * L
ROWS = 48
RHS = 33
NORM_ROW = 40
IP_ROW = 44


def split3(v):
    hi = v.astype(BF).astype(F32)
    mid = (v - hi).astype(BF).astype(F32)
    return hi, mid, v - hi - mid


def kernel(
    points, inv_scale, basis_hbm, shrink, sol, res, prev, rz,
    sol_out, res_out, dir_out,
    basis, r48, s_own, st_own, si, sj, sqj, tile,
    p_send, p_recv, p_half, e1, e2_send, e2, corr_own, corr, d48, d_own, dj,
    im_send, im_recv, im_own, e5_send, e5, c1_send, c1, c2_send, c2,
    basis_sem, ssem, rsem,
):
    row = lax.axis_index("row")
    col = lax.axis_index("col")
    core = row % 2
    y = row // 2
    z = col // 4
    x = col % 4
    xa = x // 2
    xb = ((x + 1) // 2) % 2
    g1 = z * 2 + xb
    g2 = y * 2 + xa

    def dev1(g):
        b = g % 2
        return (row, (g // 2) * 4 + 3 * xa + b - 2 * xa * b)

    def dev2(g, c):
        a = g % 2
        return ((g // 2) * 2 + c, z * 4 + 3 * a + xb - 2 * a * xb)

    other = 1 - core
    twin = (y * 2 + other, col)

    bar = pltpu.get_barrier_semaphore()
    cp = pltpu.make_async_copy(basis_hbm, basis, basis_sem)
    cp.start()
    pl.semaphore_signal(bar, inc=1, device_id=twin, device_id_type=MESH)

    def sig(s, _):
        pl.semaphore_signal(bar, inc=1, device_id=dev1((g1 + s) % G), device_id_type=MESH)
        pl.semaphore_signal(bar, inc=1, device_id=dev2((g2 + s) % G, core), device_id_type=MESH)
        pl.semaphore_signal(bar, inc=1, device_id=dev2((g2 + s) % G, other), device_id_type=MESH)
        return 0

    lax.fori_loop(1, G, sig, 0)

    def lanes(g):
        return pl.ds(pl.multiple_of(g * L, L), L)

    def send(i, src, dst, dev):
        pltpu.make_async_remote_copy(
            src_ref=src, dst_ref=dst, send_sem=ssem.at[i], recv_sem=rsem.at[i],
            device_id=dev, device_id_type=MESH,
        ).start()

    def recv_wait(i, ref):
        pltpu.make_async_copy(ref, ref, rsem.at[i]).wait()

    def send_wait(i, ref):
        pltpu.make_async_copy(ref, ref, ssem.at[i]).wait()

    inv_col = jnp.broadcast_to(inv_scale[...], (L, L)).T
    scaled = (points[...].astype(F32) * inv_col).astype(BF)
    s_own[...] = scaled
    st_own[...] = scaled.astype(F32).T.astype(BF)
    si[0, :, lanes(g1)] = s_own[...]
    sj[lanes(g2), :] = st_own[...]

    r48[...] = jnp.zeros((ROWS, L), F32)
    r48[0:RHS, :] = res[...]
    r = r48[...]
    r_bf = r.astype(BF)
    rid = lax.broadcasted_iota(jnp.int32, (ROWS, L), 0)
    lid = lax.broadcasted_iota(jnp.int32, (ROWS, L), 1)
    eye = rid == lid

    def to_row(c):
        return jnp.sum(jnp.where(eye, c, 0.0), axis=0, keepdims=True)

    def to_col(v):
        return jnp.sum(jnp.where(eye, v, 0.0), axis=1, keepdims=True)

    norm_row = to_row(jnp.sum(r * r, axis=1, keepdims=True))
    norm_in = jnp.where(rid == NORM_ROW, norm_row, 0.0)

    W = 256
    cp.wait()

    def proj_twin(n, _):
        o = pl.multiple_of(other * HALF + n * W, W)
        p_send[:, pl.ds(pl.multiple_of(n * W, W), W)] = jnp.dot(
            r_bf, basis[:, pl.ds(o, W)], preferred_element_type=F32
        )
        return 0

    lax.fori_loop(0, HALF // W, proj_twin, 0)
    for g in range(G):
        blk = p_send[:, g * L : (g + 1) * L]
        p_send[:, g * L : (g + 1) * L] = blk + norm_in

    pl.semaphore_wait(bar, 3 * (G - 1) + 1)
    send(0, p_send, p_recv, twin)

    def proj_own(n, _):
        o = pl.multiple_of(core * HALF + n * W, W)
        d = pl.ds(pl.multiple_of(n * W, W), W)
        im_own[:, d] = jnp.dot(r_bf, basis[:, pl.ds(o, W)], preferred_element_type=F32)
        return 0

    lax.fori_loop(0, HALF // W, proj_own, 0)
    recv_wait(0, p_recv)
    for g in range(G):
        d = slice(g * L, (g + 1) * L)
        v = im_own[:, d] + p_recv[:, d] + norm_in
        nrow = v[NORM_ROW : NORM_ROW + 1, :]
        hi, mid, lo = split3(nrow)
        v = jnp.where(rid == NORM_ROW, hi, v)
        v = jnp.where(rid == NORM_ROW + 1, mid, v)
        v = jnp.where(rid == NORM_ROW + 2, lo, v)
        p_half[:, d] = v.astype(BF)

    def send1(s, _):
        g = (g1 + s) % G
        send(1, p_half.at[:, lanes(g)], e1.at[g1], dev1(g))
        return 0

    lax.fori_loop(1, G, send1, 0)

    def send_pts(s, _):
        ga = (g1 + s) % G
        gb = (g2 + s) % G
        send(2, s_own, si.at[0, :, lanes(g1)], dev1(ga))
        send(3, st_own, sj.at[lanes(g2), :], dev2(gb, core))
        return 0

    lax.fori_loop(1, G, send_pts, 0)

    e1[g1] = p_half[:, lanes(g1)]
    recv_wait(1, e1.at[pl.ds(0, G - 1)])

    def resplit(v):
        n = jnp.sum(jnp.where((rid >= NORM_ROW) & (rid < NORM_ROW + 3), v, 0.0), axis=0, keepdims=True)
        return n

    acc = e1[0].astype(F32)
    for g in range(1, G):
        acc = acc + e1[g].astype(F32)
    hi, mid, lo = split3(resplit(acc))
    acc = jnp.where(rid == NORM_ROW, hi, acc)
    acc = jnp.where(rid == NORM_ROW + 1, mid, acc)
    acc = jnp.where(rid == NORM_ROW + 2, lo, acc)
    e2_send[...] = acc.astype(BF)

    def send2(s, _):
        send(4, e2_send, e2.at[g2], dev2((g2 + s) % G, core))
        return 0

    lax.fori_loop(1, G, send2, 0)
    e2[g2] = e2_send[...]
    recv_wait(4, e2.at[pl.ds(0, G - 1)])
    acc = e2[0].astype(F32)
    for g in range(1, G):
        acc = acc + e2[g].astype(F32)
    norm_tot = resplit(acc)
    damping = shrink[pl.ds(core * G + g1, 1), :] - 1.0
    proj = jnp.where(rid < RHS, acc, 0.0)
    cor = (damping * proj).astype(BF)
    ip = to_row(jnp.sum(cor.astype(F32) * proj, axis=1, keepdims=True))
    hi, mid, lo = split3(ip)
    cf = cor.astype(F32)
    cf = jnp.where(rid == IP_ROW, hi, cf)
    cf = jnp.where(rid == IP_ROW + 1, mid, cf)
    cf = jnp.where(rid == IP_ROW + 2, lo, cf)
    corr_own[...] = cf.astype(BF)

    def send3(s, _):
        send(5, corr_own, corr.at[:, lanes(core * G + g1)], dev1((g1 + s) % G))
        return 0

    lax.fori_loop(1, G, send3, 0)
    corr[:, lanes(core * G + g1)] = corr_own[...]

    recv_wait(2, si.at[0, :, pl.ds(0, HALF - L)])
    recv_wait(3, sj.at[pl.ds(0, HALF - L), :])
    send(6, si.at[0], si.at[1], twin)

    recv_wait(5, corr.at[:, pl.ds(0, HALF - L)])
    half = corr.at[:, pl.ds(pl.multiple_of(core * HALF, HALF), HALF)]
    send(7, half, half, twin)

    def sq_rows(n, _):
        d = lanes(n)
        v = sj[d, :].astype(F32)
        sqj[d, :] = jnp.broadcast_to(0.5 * jnp.sum(v * v, axis=1, keepdims=True), (L, L))
        return 0

    lax.fori_loop(0, G, sq_rows, 0)

    def build(h):
        def outer(n, _):
            d = pl.ds(pl.multiple_of(n * W, W), W)
            pts = si[h, :, d]
            pf = pts.astype(F32)
            sq = 0.5 * jnp.sum(pf * pf, axis=0, keepdims=True)

            def inner(m, _):
                e = pl.ds(pl.multiple_of(m * W, W), W)
                cross = jnp.dot(sj[e, :], pts, preferred_element_type=F32)
                sc = sqj[e, :]
                sc = jnp.concatenate([sc, sc], axis=1)
                tile[h, e, d] = jnp.exp(jnp.minimum(cross - sc - sq, 0.0)).astype(BF)
                return 0

            lax.fori_loop(0, HALF // W, inner, 0)
            return 0

        lax.fori_loop(0, HALF // W, outer, 0)

    build(0)

    recv_wait(7, half)
    full = corr[...]
    ipr = jnp.zeros((1, L), F32)
    for g in range(2 * G):
        blk = corr[IP_ROW : IP_ROW + 3, g * L : (g + 1) * L].astype(F32)
        ipr = ipr + jnp.sum(blk, axis=0, keepdims=True)
    ip_col = to_col(ipr + norm_tot)
    cid = lax.broadcasted_iota(jnp.int32, (ROWS, 1), 0)
    rzp = jnp.concatenate([rz[...], jnp.ones((1, L - RHS), F32)], axis=1)
    rz_col = jnp.where(cid < RHS, to_col(rzp), 1.0)
    pre = r + lax.dot_general(full, basis[...], (((1,), (1,)), ((), ())), preferred_element_type=F32)
    d48[...] = jnp.zeros((ROWS, L), F32)
    d48[0:RHS, :] = prev[...]
    direction = pre + (ip_col / rz_col) * d48[...]
    direction = jnp.where(rid < RHS, direction, 0.0)
    d48[...] = direction
    d_own[...] = direction.astype(BF)

    def send4(s, _):
        send(8, d_own, dj.at[:, lanes(g2)], dev2((g2 + s) % G, core))
        return 0

    lax.fori_loop(1, G, send4, 0)
    dj[:, lanes(g2)] = d_own[...]

    recv_wait(6, si.at[1])
    build(1)
    recv_wait(8, dj.at[:, pl.ds(0, HALF - L)])

    def image(h, out):
        def step(n, _):
            d = pl.ds(pl.multiple_of(n * W, W), W)
            out[:, d] = jnp.dot(dj[...], tile[h, :, d], preferred_element_type=F32)
            return 0

        lax.fori_loop(0, HALF // W, step, 0)

    image(1, im_send)
    send(9, im_send, im_recv, twin)
    image(0, im_own)
    recv_wait(9, im_recv)
    e5_send[...] = (im_own[...] + im_recv[...]).astype(BF)

    def send5(s, _):
        g = (g1 + s) % G
        send(10, e5_send.at[:, lanes(g)], e5.at[g1], dev1(g))
        return 0

    lax.fori_loop(1, G, send5, 0)
    e5[g1] = e5_send[:, lanes(g1)]
    recv_wait(10, e5.at[pl.ds(0, G - 1)])
    acc = e5[0].astype(F32)
    for g in range(1, G):
        acc = acc + e5[g].astype(F32)
    direction = d48[...]
    img = acc + NOISE * direction

    cur = to_row(jnp.sum(direction * img, axis=1, keepdims=True))
    c1_send[...] = jnp.broadcast_to(cur, (8, L))

    def send6(s, _):
        send(11, c1_send, c1.at[g1], dev1((g1 + s) % G))
        return 0

    lax.fori_loop(1, G, send6, 0)
    c1[g1] = c1_send[...]
    recv_wait(11, c1.at[pl.ds(0, G - 1)])
    c2_send[...] = jnp.sum(c1[...], axis=0)

    def send7(s, _):
        g = (g2 + s) % G
        send(12, c2_send, c2.at[core * G + g2], dev2(g, core))
        send(12, c2_send, c2.at[core * G + g2], dev2(g, other))
        return 0

    send(12, c2_send, c2.at[core * G + g2], twin)
    lax.fori_loop(1, G, send7, 0)
    c2[core * G + g2] = c2_send[...]
    recv_wait(12, c2.at[pl.ds(0, 2 * G - 1)])
    cur = jnp.sum(c2[...], axis=0)[0:1, :]
    cur_col = jnp.where(cid < RHS, to_col(cur), 1.0)
    alpha = ip_col / cur_col
    dir_out[...] = direction[0:RHS, :]
    sol_out[...] = sol[...] + (alpha * direction)[0:RHS, :]
    res_out[...] = res[...] - (alpha * img)[0:RHS, :]

    send_wait(0, p_send)
    send_wait(1, e1.at[pl.ds(0, G - 1)])
    send_wait(2, si.at[0, :, pl.ds(0, HALF - L)])
    send_wait(3, sj.at[pl.ds(0, HALF - L), :])
    send_wait(4, e2.at[pl.ds(0, G - 1)])
    send_wait(5, corr.at[:, pl.ds(0, HALF - L)])
    send_wait(6, si.at[0])
    send_wait(7, half)
    send_wait(8, dj.at[:, pl.ds(0, HALF - L)])
    send_wait(9, im_send)
    send_wait(10, e5.at[pl.ds(0, G - 1)])
    send_wait(11, c1.at[pl.ds(0, G - 1)])
    send_wait(12, c2.at[pl.ds(0, 2 * G - 1)])


def solution(mesh):
    axes = ("row", "col")
    pts = P(None, axes)
    placed = (pts, P(), P(axes, None), P(), pts, pts, pts, P())

    def step(points, inv_scale, basis, shrink, sol, res, prev, rz):
        rank = basis.shape[1]
        out = jax.ShapeDtypeStruct((RHS, L), F32)
        v = pl.BlockSpec(memory_space=pltpu.VMEM)
        return pl.pallas_call(
            kernel,
            out_shape=(out, out, out),
            in_specs=[v, v, pl.BlockSpec(memory_space=pl.ANY), v, v, v, v, v],
            out_specs=(v, v, v),
            scratch_shapes=[
                pltpu.VMEM((L, rank), BF),
                pltpu.VMEM((ROWS, L), F32),
                pltpu.VMEM((L, L), BF),
                pltpu.VMEM((L, L), BF),
                pltpu.VMEM((2, L, HALF), BF),
                pltpu.VMEM((HALF, L), BF),
                pltpu.VMEM((HALF, L), F32),
                pltpu.VMEM((2, HALF, HALF), BF),
                pltpu.VMEM((ROWS, HALF), F32),
                pltpu.VMEM((ROWS, HALF), F32),
                pltpu.VMEM((ROWS, HALF), BF),
                pltpu.VMEM((G, ROWS, L), BF),
                pltpu.VMEM((ROWS, L), BF),
                pltpu.VMEM((G, ROWS, L), BF),
                pltpu.VMEM((ROWS, L), BF),
                pltpu.VMEM((ROWS, rank), BF),
                pltpu.VMEM((ROWS, L), F32),
                pltpu.VMEM((ROWS, L), BF),
                pltpu.VMEM((ROWS, HALF), BF),
                pltpu.VMEM((ROWS, HALF), F32),
                pltpu.VMEM((ROWS, HALF), F32),
                pltpu.VMEM((ROWS, HALF), F32),
                pltpu.VMEM((ROWS, HALF), BF),
                pltpu.VMEM((G, ROWS, L), BF),
                pltpu.VMEM((8, L), F32),
                pltpu.VMEM((G, 8, L), F32),
                pltpu.VMEM((8, L), F32),
                pltpu.VMEM((2 * G, 8, L), F32),
                pltpu.SemaphoreType.DMA,
                pltpu.SemaphoreType.DMA((13,)),
                pltpu.SemaphoreType.DMA((13,)),
            ],
            compiler_params=pltpu.CompilerParams(
                collective_id=0, has_side_effects=True, vmem_limit_bytes=48 * 1024 * 1024
            ),
            name="cg_step",
        )(
            points, inv_scale.reshape(1, L), basis, shrink.reshape(rank // L, L),
            sol, res, prev, rz.reshape(1, RHS),
        )

    return jax.shard_map(
        step, mesh=mesh, in_specs=placed, out_specs=(pts, pts, pts), check_vma=False
    )
```

```python
import jax
import jax.numpy as jnp
from jax import lax
from jax.experimental import pallas as pl
from jax.experimental.pallas import tpu as pltpu
from jax.sharding import PartitionSpec as P

MESH = pl.DeviceIdType.MESH
BF = jnp.bfloat16
F32 = jnp.float32
NOISE = 0.25
G = 16
L = 128
HALF = G * L
RHS = 33
ROWS = 40
NORM = 33
INNER = 36


def split3(v):
    hi = v.astype(BF).astype(F32)
    mid = (v - hi).astype(BF).astype(F32)
    return hi, mid, v - hi - mid


def kernel(
    points, inv_scale, basis_hbm, shrink, res, prev, rz,
    pre_out, beta_out, alpha_out, img_out,
    basis, r40, s_own, st_own, si, sj, tile,
    p_send, p_recv, p_half, e1, e2_send, e2, corr_own, corr, d40, d_own, dj, di,
    im_send, im_recv, im_own, e5_send, e5, c2_send, c2, c3_send, c3,
    basis_sem, ssem, rsem,
):
    row = lax.axis_index("row")
    col = lax.axis_index("col")
    core = row % 2
    y = row // 2
    z = col // 4
    x = col % 4
    xa = x // 2
    xb = ((x + 1) // 2) % 2
    g1 = z * 2 + xb
    g2 = y * 2 + xa
    other = 1 - core
    twin = (y * 2 + other, col)

    def far(t):
        return (4 + ((t + 1) // 2) * (1 - 2 * (t % 2))) % 8

    def dev1(t, flip):
        zz = (z + far(t)) % 8
        b = (xb + flip) % 2
        return (row, zz * 4 + 3 * xa + b - 2 * xa * b), zz * 2 + b

    def dev2(t, flip):
        yy = (y + far(t)) % 8
        a = (xa + flip) % 2
        return (yy * 2 + core, z * 4 + 3 * a + xb - 2 * a * xb), yy * 2 + a

    def each(dev, fn, lo=0, hi=8):
        def body(t, _):
            fn(*dev(t, 1))
            fn(*dev(t, 0))
            return 0

        lax.fori_loop(lo, min(hi, 7), body, 0)
        if hi == 8:
            fn(*dev(7, 1))

    def lanes(g):
        return pl.ds(pl.multiple_of(g * L, L), L)

    def send(i, src, dst, dev):
        pltpu.make_async_remote_copy(
            src_ref=src, dst_ref=dst, send_sem=ssem.at[i], recv_sem=rsem.at[i],
            device_id=dev, device_id_type=MESH,
        ).start()

    sent, coming = {}, {}

    def expect(i, ref):
        sent[i] = ref
        coming[i] = ref

    def recv_wait(i):
        ref = coming.pop(i)
        pltpu.make_async_copy(ref, ref, rsem.at[i]).wait()

    def drain():
        for i in list(coming):
            recv_wait(i)
        for i, ref in sent.items():
            pltpu.make_async_copy(ref, ref, ssem.at[i]).wait()

    bar = pltpu.get_barrier_semaphore()
    cp = pltpu.make_async_copy(basis_hbm, basis, basis_sem)
    cp.start()

    def signal(dev, _):
        pl.semaphore_signal(bar, inc=1, device_id=dev, device_id_type=MESH)

    signal(twin, 0)
    each(dev1, signal)
    each(dev2, signal)

    inv_col = jnp.broadcast_to(inv_scale[...], (L, L)).T
    scaled = (points[...].astype(F32) * inv_col).astype(BF)
    s_own[...] = scaled
    st_own[...] = scaled.astype(F32).T.astype(BF)
    si[0, 0:L, lanes(g1)] = s_own[...]
    sj[lanes(g2), 0:L] = st_own[...]
    for h in range(2):
        si[h, L : 2 * L, :] = jnp.zeros((L, HALF), BF)

    r40[...] = jnp.zeros((ROWS, L), F32)
    r40[0:RHS, :] = res[...]
    r = r40[...]
    r_bf = r.astype(BF)
    rid = lax.broadcasted_iota(jnp.int32, (ROWS, L), 0)
    lid = lax.broadcasted_iota(jnp.int32, (ROWS, L), 1)
    cid = lax.broadcasted_iota(jnp.int32, (ROWS, 1), 0)
    eye = rid == lid

    def to_row(c):
        return jnp.sum(jnp.where(eye, c, 0.0), axis=0, keepdims=True)

    def to_col(v):
        return jnp.sum(jnp.where(eye, v, 0.0), axis=1, keepdims=True)

    def put(v, base, line):
        hi, mid, lo = split3(line)
        v = jnp.where(rid == base, hi, v)
        v = jnp.where(rid == base + 1, mid, v)
        return jnp.where(rid == base + 2, lo, v)

    def take(v, base):
        return jnp.sum(jnp.where((rid >= base) & (rid < base + 3), v, 0.0), axis=0, keepdims=True)

    zero = jnp.zeros((ROWS, L), F32)
    norm = to_row(jnp.sum(r * r, axis=1, keepdims=True))
    norm_in = put(zero, NORM, norm)

    cp.wait()

    def half_of(c):
        return pl.ds(pl.multiple_of(c * HALF, HALF), HALF)

    proj_t = jnp.dot(r_bf, basis[:, half_of(other)], preferred_element_type=F32)
    for g in range(G):
        d = slice(g * L, (g + 1) * L)
        p_send[:, d] = (proj_t[:, d] + norm_in).astype(BF)
    im_own[...] = jnp.dot(r_bf, basis[:, half_of(core)], preferred_element_type=F32)

    pl.semaphore_wait(bar, 2 * (G - 1) + 1)
    send(0, p_send, p_recv, twin)
    expect(0, p_send)

    def send_j(dev, g):
        send(3, st_own, sj.at[lanes(g2), pl.ds(0, L)], dev)

    def send_i(dev, g):
        send(2, s_own, si.at[0, pl.ds(0, L), lanes(g1)], dev)

    each(dev2, send_j)
    expect(3, sj.at[pl.ds(0, HALF - L), pl.ds(0, L)])
    each(dev1, send_i, 5, 8)
    expect(2, si.at[0, pl.ds(0, L), pl.ds(0, HALF - L)])

    recv_wait(0)
    norm_in = put(zero, NORM, norm + take(p_recv[:, 0:L].astype(F32), NORM))
    for g in range(G):
        d = slice(g * L, (g + 1) * L)
        v = im_own[:, d] + p_recv[:, d].astype(F32)
        p_half[:, d] = jnp.where(rid < RHS, v, norm_in).astype(BF)

    def send1(dev, g):
        send(1, p_half.at[:, lanes(g)], e1.at[g1], dev)

    each(dev1, send1)
    expect(1, e1.at[pl.ds(0, G - 1)])
    e1[g1] = p_half[:, lanes(g1)]

    def total(ref):
        acc = ref[0].astype(F32)
        for g in range(1, G):
            acc = acc + ref[g].astype(F32)
        return acc

    recv_wait(1)
    acc = total(e1)
    e2_send[...] = put(acc, NORM, take(acc, NORM)).astype(BF)

    def send2(dev, g):
        send(4, e2_send, e2.at[g2], dev)

    each(dev2, send2)
    expect(4, e2.at[pl.ds(0, G - 1)])
    each(dev1, send_i, 0, 5)
    e2[g2] = e2_send[...]
    recv_wait(4)
    acc = total(e2)
    norm_all = take(acc, NORM)
    proj = jnp.where(rid < RHS, acc, 0.0)
    cor = ((shrink[pl.ds(core * G + g1, 1), :] - 1.0) * proj).astype(BF).astype(F32)
    inner = to_row(jnp.sum(cor * proj, axis=1, keepdims=True))
    corr_own[...] = put(cor, INNER, inner).astype(BF)

    def send3(dev, g):
        send(5, corr_own, corr.at[:, lanes(core * G + g1)], dev)

    each(dev1, send3)
    expect(5, corr.at[:, pl.ds(0, HALF - L)])
    corr[:, lanes(core * G + g1)] = corr_own[...]

    lane = lax.broadcasted_iota(jnp.int32, (L, L), 1)

    def aug_j():
        def body(n, _):
            v = sj[lanes(n), 0:L].astype(F32)
            hi, mid, lo = split3(jnp.broadcast_to(-0.5 * jnp.sum(v * v, axis=1, keepdims=True), (L, L)))
            ext = jnp.where(lane == 0, hi, jnp.where(lane == 1, mid, jnp.where(lane == 2, lo, 1.0)))
            sj[lanes(n), L : 2 * L] = jnp.where(lane < 6, ext, 0.0).astype(BF)
            return 0

        lax.fori_loop(0, G, body, 0)

    def aug_i(h):
        W = 512
        line = lax.broadcasted_iota(jnp.int32, (16, W), 0)

        def body(n, _):
            d = pl.ds(pl.multiple_of(n * W, W), W)
            v = si[h, 0:L, d].astype(F32)
            hi, mid, lo = split3(-0.5 * jnp.sum(v * v, axis=0, keepdims=True))
            ext = jnp.where(line == 3, hi, jnp.where(line == 4, mid, jnp.where(line == 5, lo, 1.0)))
            si[h, L : L + 16, d] = jnp.where(line < 6, ext, 0.0).astype(BF)
            return 0

        lax.fori_loop(0, HALF // W, body, 0)

    def build(h):
        M, W = 1024, 512

        def body(n, _):
            d = pl.ds(pl.multiple_of(n * W, W), W)
            pts = si[h, :, d]
            for m in range(HALF // M):
                e = slice(m * M, (m + 1) * M)
                neg = jnp.dot(sj[e, :], pts, preferred_element_type=F32)
                tile[h, e, d] = jnp.exp(jnp.minimum(neg, 0.0)).astype(BF)
            return 0

        lax.fori_loop(0, HALF // W, body, 0)

    recv_wait(3)
    aug_j()
    recv_wait(2)
    send(6, si.at[0, pl.ds(0, L)], si.at[1, pl.ds(0, L)], twin)
    expect(6, si.at[0, pl.ds(0, L)])
    aug_i(0)
    build(0)
    recv_wait(5)
    half = corr.at[:, half_of(core)]
    send(7, half, half, twin)
    expect(7, half)

    def apply(c):
        return lax.dot_general(
            corr[:, half_of(c)], basis[:, half_of(c)], (((1,), (1,)), ((), ())),
            preferred_element_type=F32,
        )

    pre = r + apply(core)
    d40[...] = zero
    d40[0:RHS, :] = prev[...]
    rz_row = jnp.concatenate([rz[...], jnp.ones((1, L - RHS), F32)], axis=1)
    rz_col = jnp.where(cid < RHS, to_col(rz_row), 1.0)
    recv_wait(7)
    pre = pre + apply(other)
    tail = corr[32:ROWS, 0:L].astype(F32)
    for g in range(1, 2 * G):
        tail = tail + corr[32:ROWS, g * L : (g + 1) * L].astype(F32)
    tid = lax.broadcasted_iota(jnp.int32, (8, L), 0)
    keep = (tid >= INNER - 32) & (tid < INNER - 29)
    inner = jnp.sum(jnp.where(keep, tail, 0.0), axis=0, keepdims=True)
    inner_col = to_col(inner + norm_all)
    beta = inner_col / rz_col
    direction = jnp.where(rid < RHS, pre + beta * d40[...], 0.0)
    d40[...] = direction
    d_own[...] = direction.astype(BF)

    def send4(dev, g):
        send(8, d_own, dj.at[:, lanes(g2)], dev)

    def send5(dev, g):
        send(9, d_own, di.at[:, lanes(g1)], dev)

    each(dev2, send4)
    each(dev1, send5)
    expect(8, dj.at[:, pl.ds(0, HALF - L)])
    expect(9, di.at[:, pl.ds(0, HALF - L)])
    dj[:, lanes(g2)] = d_own[...]
    di[:, lanes(g1)] = d_own[...]
    pre_out[...] = pre[0:RHS, :]
    beta_out[...] = jnp.broadcast_to(beta, (ROWS, L))[0:RHS, :]
    own_curv = NOISE * jnp.sum(direction * direction, axis=1, keepdims=True)

    recv_wait(6)
    aug_i(1)
    build(1)
    recv_wait(8)

    def image(h, out):
        W = 1024
        for n in range(HALF // W):
            d = slice(n * W, (n + 1) * W)
            out[:, d] = jnp.dot(dj[...], tile[h, :, d], preferred_element_type=F32).astype(out.dtype)

    image(1, im_send)
    send(10, im_send, im_recv, twin)
    expect(10, im_send)
    image(0, im_own)
    recv_wait(9)
    recv_wait(10)
    curv = zero
    for g in range(G):
        d = slice(g * L, (g + 1) * L)
        v = im_own[:, d] + im_recv[:, d].astype(F32)
        im_own[:, d] = v
        curv = curv + v * di[:, d].astype(F32)
    curv = to_row(jnp.sum(curv, axis=1, keepdims=True) + own_curv)
    curv_in = put(zero, NORM, curv)
    for g in range(G):
        d = slice(g * L, (g + 1) * L)
        e5_send[:, d] = (im_own[:, d] + curv_in).astype(BF)

    def send6(dev, g):
        send(11, e5_send.at[:, lanes(g)], e5.at[g1], dev)

    each(dev1, send6)
    expect(11, e5.at[pl.ds(0, G - 1)])
    e5[g1] = e5_send[:, lanes(g1)]
    recv_wait(11)
    acc = total(e5)
    c2_send[...] = take(acc, NORM)

    def send7(dev, g):
        send(12, c2_send, c2.at[g2], dev)

    each(dev2, send7)
    expect(12, c2.at[pl.ds(0, G - 1)])
    c2[g2] = c2_send[...]
    img_out[...] = (acc + NOISE * d40[...])[0:RHS, :]
    recv_wait(12)
    c3_send[...] = jnp.sum(c2[...], axis=0)
    send(13, c3_send, c3, twin)
    expect(13, c3_send)
    recv_wait(13)
    curv_col = jnp.where(cid < RHS, to_col(c3_send[...] + c3[...]), 1.0)
    alpha = inner_col / curv_col
    alpha_out[...] = jnp.broadcast_to(alpha, (ROWS, L))[0:RHS, :]
    drain()


def solution(mesh):
    axes = ("row", "col")
    pts = P(None, axes)
    placed = (pts, P(), P(axes, None), P(), pts, pts, pts, P())

    def step(points, inv_scale, basis, shrink, sol, res, prev, rz):
        rank = basis.shape[1]
        out = jax.ShapeDtypeStruct((RHS, L), F32)
        v = pl.BlockSpec(memory_space=pltpu.VMEM)
        pre, beta, alpha, img = pl.pallas_call(
            kernel,
            out_shape=(out,) * 4,
            in_specs=[v, v, pl.BlockSpec(memory_space=pl.ANY), v, v, v, v],
            out_specs=(v,) * 4,
            scratch_shapes=[
                pltpu.VMEM((L, rank), BF),
                pltpu.VMEM((ROWS, L), F32),
                pltpu.VMEM((L, L), BF),
                pltpu.VMEM((L, L), BF),
                pltpu.VMEM((2, 2 * L, HALF), BF),
                pltpu.VMEM((HALF, 2 * L), BF),
                pltpu.VMEM((2, HALF, HALF), BF),
                pltpu.VMEM((ROWS, HALF), BF),
                pltpu.VMEM((ROWS, HALF), BF),
                pltpu.VMEM((ROWS, HALF), BF),
                pltpu.VMEM((G, ROWS, L), BF),
                pltpu.VMEM((ROWS, L), BF),
                pltpu.VMEM((G, ROWS, L), BF),
                pltpu.VMEM((ROWS, L), BF),
                pltpu.VMEM((ROWS, rank), BF),
                pltpu.VMEM((ROWS, L), F32),
                pltpu.VMEM((ROWS, L), BF),
                pltpu.VMEM((ROWS, HALF), BF),
                pltpu.VMEM((ROWS, HALF), BF),
                pltpu.VMEM((ROWS, HALF), BF),
                pltpu.VMEM((ROWS, HALF), BF),
                pltpu.VMEM((ROWS, HALF), F32),
                pltpu.VMEM((ROWS, HALF), BF),
                pltpu.VMEM((G, ROWS, L), BF),
                pltpu.VMEM((1, L), F32),
                pltpu.VMEM((G, 1, L), F32),
                pltpu.VMEM((1, L), F32),
                pltpu.VMEM((1, L), F32),
                pltpu.SemaphoreType.DMA,
                pltpu.SemaphoreType.DMA((14,)),
                pltpu.SemaphoreType.DMA((14,)),
            ],
            compiler_params=pltpu.CompilerParams(
                collective_id=0, has_side_effects=True, vmem_limit_bytes=62 * 1024 * 1024
            ),
            name="cg_step",
        )(
            points, inv_scale.reshape(1, L), basis, shrink.reshape(rank // L, L),
            res, prev, rz.reshape(1, RHS),
        )
        direction = pre + beta * prev
        return sol + alpha * direction, res - alpha * img, direction

    return jax.shard_map(
        step, mesh=mesh, in_specs=placed, out_specs=(pts, pts, pts), check_vma=False
    )
```

```python
import jax
import jax.numpy as jnp
from jax import lax
from jax.experimental import pallas as pl
from jax.experimental.pallas import tpu as pltpu
from jax.sharding import PartitionSpec as P

MESH = pl.DeviceIdType.MESH
BF = jnp.bfloat16
F32 = jnp.float32
NOISE = 0.25
G = 16
L = 128
HALF = G * L
RHS = 33
ROWS = 40
NORM = 33
INNER = 36


def split3(v):
    hi = v.astype(BF).astype(F32)
    mid = (v - hi).astype(BF).astype(F32)
    return hi, mid, v - hi - mid


def kernel(
    points, inv_scale, basis_hbm, shrink, res, prev, rz,
    pre_out, beta_out, alpha_out, img_out,
    basis, r40, s_own, st_own, si, sj, tile,
    p_send, p_recv, p_half, e1, e2_send, e2, corr_own, corr, d40, d_own, dj, di,
    im_send, im_recv, im_own, e5_send, e5, c2_send, c2,
    basis_sem, ssem, rsem,
):
    row = lax.axis_index("row")
    col = lax.axis_index("col")
    core = row % 2
    y = row // 2
    z = col // 4
    x = col % 4
    xa = x // 2
    xb = ((x + 1) // 2) % 2
    g1 = xb * 8 + z
    g2 = y * 2 + xa
    other = 1 - core
    twin = (y * 2 + other, col)

    def far(t):
        return (4 + ((t + 1) // 2) * (1 - 2 * (t % 2))) % 8

    def dev1(t, flip):
        zz = (z + far(t)) % 8
        b = (xb + flip) % 2
        return (row, zz * 4 + 3 * xa + b - 2 * xa * b), b * 8 + zz

    def dev2(t, flip, c=core):
        yy = (y + far(t)) % 8
        a = (xa + flip) % 2
        return (yy * 2 + c, z * 4 + 3 * a + xb - 2 * a * xb), 2 * t + 1 - flip

    def each(dev, fn, lo=0, hi=8):
        def body(t, _):
            fn(*dev(t, 1))
            fn(*dev(t, 0))
            return 0

        lax.fori_loop(lo, min(hi, 7), body, 0)
        if hi == 8:
            fn(*dev(7, 1))

    def lanes(g):
        return pl.ds(pl.multiple_of(g * L, L), L)

    def send(i, src, dst, dev):
        pltpu.make_async_remote_copy(
            src_ref=src, dst_ref=dst, send_sem=ssem.at[i], recv_sem=rsem.at[i],
            device_id=dev, device_id_type=MESH,
        ).start()

    sent, coming = {}, {}

    def expect(i, ref):
        sent[i] = ref
        coming[i] = ref

    def recv_wait(i):
        ref = coming.pop(i)
        pltpu.make_async_copy(ref, ref, rsem.at[i]).wait()

    def drain():
        for i in list(coming):
            recv_wait(i)
        for i, ref in sent.items():
            pltpu.make_async_copy(ref, ref, ssem.at[i]).wait()

    bar = pltpu.get_barrier_semaphore()
    cp = pltpu.make_async_copy(basis_hbm, basis, basis_sem)
    cp.start()

    def signal(dev, _):
        pl.semaphore_signal(bar, inc=1, device_id=dev, device_id_type=MESH)

    signal(twin, 0)
    each(dev1, signal)
    each(dev2, signal)

    inv_col = jnp.broadcast_to(inv_scale[...], (L, L)).T
    scaled = (points[...].astype(F32) * inv_col).astype(BF)
    s_own[...] = scaled
    st_own[...] = scaled.astype(F32).T.astype(BF)
    si[0, 0:L, lanes(g1)] = s_own[...]
    sj[HALF - L : HALF, 0:L] = st_own[...]
    for h in range(2):
        si[h, L : 2 * L, :] = jnp.zeros((L, HALF), BF)

    r40[...] = jnp.zeros((ROWS, L), F32)
    r40[0:RHS, :] = res[...]
    r = r40[...]
    r_bf = r.astype(BF)
    rid = lax.broadcasted_iota(jnp.int32, (ROWS, L), 0)
    lid = lax.broadcasted_iota(jnp.int32, (ROWS, L), 1)
    cid = lax.broadcasted_iota(jnp.int32, (ROWS, 1), 0)
    eye = rid == lid

    def to_row(c):
        return jnp.sum(jnp.where(eye, c, 0.0), axis=0, keepdims=True)

    def to_col(v):
        return jnp.sum(jnp.where(eye, v, 0.0), axis=1, keepdims=True)

    def put(v, base, line):
        hi, mid, lo = split3(line)
        v = jnp.where(rid == base, hi, v)
        v = jnp.where(rid == base + 1, mid, v)
        return jnp.where(rid == base + 2, lo, v)

    def take(v, base):
        return jnp.sum(jnp.where((rid >= base) & (rid < base + 3), v, 0.0), axis=0, keepdims=True)

    zero = jnp.zeros((ROWS, L), F32)
    norm = to_row(jnp.sum(r * r, axis=1, keepdims=True))
    norm_in = put(zero, NORM, norm)

    cp.wait()

    def half_of(c):
        return pl.ds(pl.multiple_of(c * HALF, HALF), HALF)

    proj_t = jnp.dot(r_bf, basis[:, half_of(other)], preferred_element_type=F32)
    for g in range(G):
        d = slice(g * L, (g + 1) * L)
        p_send[:, d] = (proj_t[:, d] + norm_in).astype(BF)
    im_own[...] = jnp.dot(r_bf, basis[:, half_of(core)], preferred_element_type=F32)

    pl.semaphore_wait(bar, 2 * (G - 1) + 1)
    send(0, p_send, p_recv, twin)
    expect(0, p_send)

    def send_j(dev, g):
        send(3, st_own, sj.at[lanes(g), pl.ds(0, L)], dev)

    def send_i():
        def body(t, _):
            send(2, s_own, si.at[0, pl.ds(0, L), lanes(g1)], dev1(t, 0)[0])
            return 0

        lax.fori_loop(0, 7, body, 0)
        expect(2, si.at[0, pl.ds(0, L), pl.ds(0, 7 * L)])

    each(dev2, send_j)
    expect(3, sj.at[pl.ds(0, HALF - L), pl.ds(0, L)])
    send_i()

    recv_wait(0)
    norm_in = put(zero, NORM, norm + take(p_recv[:, 0:L].astype(F32), NORM))
    for g in range(G):
        d = slice(g * L, (g + 1) * L)
        v = im_own[:, d] + p_recv[:, d].astype(F32)
        p_half[:, d] = jnp.where(rid < RHS, v, norm_in).astype(BF)

    def send1(dev, g):
        send(1, p_half.at[:, lanes(g)], e1.at[g1], dev)

    each(dev1, send1)
    expect(1, e1.at[pl.ds(0, G - 1)])
    e1[g1] = p_half[:, lanes(g1)]

    def total(ref):
        acc = ref[0].astype(F32)
        for g in range(1, G):
            acc = acc + ref[g].astype(F32)
        return acc

    recv_wait(1)
    acc = total(e1)
    e2_send[...] = put(acc, NORM, take(acc, NORM)).astype(BF)

    def send2(dev, g):
        send(4, e2_send, e2.at[g2], dev)

    each(dev2, send2)
    expect(4, e2.at[pl.ds(0, G - 1)])
    recv_wait(2)
    relay = si.at[0, pl.ds(0, L), pl.ds(pl.multiple_of(xb * 8 * L, 8 * L), 8 * L)]
    send(14, relay, relay, dev1(7, 1)[0])
    expect(14, relay)
    e2[g2] = e2_send[...]
    recv_wait(4)
    acc = total(e2)
    norm_all = take(acc, NORM)
    proj = jnp.where(rid < RHS, acc, 0.0)
    cor = ((shrink[pl.ds(core * G + g1, 1), :] - 1.0) * proj).astype(BF).astype(F32)
    inner = to_row(jnp.sum(cor * proj, axis=1, keepdims=True))
    corr_own[...] = put(cor, INNER, inner).astype(BF)

    def send3(dev, g):
        send(5, corr_own, corr.at[:, lanes(core * G + g1)], dev)

    each(dev1, send3)
    expect(5, corr.at[:, pl.ds(0, HALF - L)])
    corr[:, lanes(core * G + g1)] = corr_own[...]

    lane = lax.broadcasted_iota(jnp.int32, (L, L), 1)

    def aug_j():
        def body(n, _):
            v = sj[lanes(n), 0:L].astype(F32)
            hi, mid, lo = split3(jnp.broadcast_to(-0.5 * jnp.sum(v * v, axis=1, keepdims=True), (L, L)))
            ext = jnp.where(lane == 0, hi, jnp.where(lane == 1, mid, jnp.where(lane == 2, lo, 1.0)))
            sj[lanes(n), L : 2 * L] = jnp.where(lane < 6, ext, 0.0).astype(BF)
            return 0

        lax.fori_loop(0, G, body, 0)

    def aug_i(h):
        W = 512
        line = lax.broadcasted_iota(jnp.int32, (16, W), 0)

        def body(n, _):
            d = pl.ds(pl.multiple_of(n * W, W), W)
            v = si[h, 0:L, d].astype(F32)
            hi, mid, lo = split3(-0.5 * jnp.sum(v * v, axis=0, keepdims=True))
            ext = jnp.where(line == 3, hi, jnp.where(line == 4, mid, jnp.where(line == 5, lo, 1.0)))
            si[h, L : L + 16, d] = jnp.where(line < 6, ext, 0.0).astype(BF)
            return 0

        lax.fori_loop(0, HALF // W, body, 0)

    def build(h):
        M, W = 1024, 512

        def body(n, _):
            d = pl.ds(pl.multiple_of(n * W, W), W)
            pts = si[h, :, d]
            for m in range(HALF // M):
                e = slice(m * M, (m + 1) * M)
                neg = jnp.dot(sj[e, :], pts, preferred_element_type=F32)
                tile[h, e, d] = jnp.exp(jnp.minimum(neg, 0.0)).astype(BF)
            return 0

        lax.fori_loop(0, HALF // W, body, 0)

    recv_wait(3)
    aug_j()
    recv_wait(14)
    send(6, si.at[0, pl.ds(0, L)], si.at[1, pl.ds(0, L)], twin)
    expect(6, si.at[0, pl.ds(0, L)])
    aug_i(0)
    build(0)
    recv_wait(5)
    half = corr.at[:, half_of(core)]
    send(7, half, half, twin)
    expect(7, half)

    def apply(c):
        return lax.dot_general(
            corr[:, half_of(c)], basis[:, half_of(c)], (((1,), (1,)), ((), ())),
            preferred_element_type=F32,
        )

    pre = r + apply(core)
    d40[...] = zero
    d40[0:RHS, :] = prev[...]
    rz_row = jnp.concatenate([rz[...], jnp.ones((1, L - RHS), F32)], axis=1)
    rz_col = jnp.where(cid < RHS, to_col(rz_row), 1.0)
    recv_wait(7)
    pre = pre + apply(other)
    tail = corr[32:ROWS, 0:L].astype(F32)
    for g in range(1, 2 * G):
        tail = tail + corr[32:ROWS, g * L : (g + 1) * L].astype(F32)
    tid = lax.broadcasted_iota(jnp.int32, (8, L), 0)
    keep = (tid >= INNER - 32) & (tid < INNER - 29)
    inner = jnp.sum(jnp.where(keep, tail, 0.0), axis=0, keepdims=True)
    inner_col = to_col(inner + norm_all)
    beta = inner_col / rz_col
    direction = jnp.where(rid < RHS, pre + beta * d40[...], 0.0)
    d40[...] = direction
    d_own[...] = direction.astype(BF)

    def send4(dev, g):
        send(8, d_own, dj.at[:, lanes(g)], dev)

    def send5(dev, g):
        send(9, d_own, di.at[:, lanes(g1)], dev)

    each(dev2, send4)
    each(dev1, send5)
    expect(8, dj.at[:, pl.ds(0, HALF - L)])
    expect(9, di.at[:, pl.ds(0, HALF - L)])
    dj[:, HALF - L : HALF] = d_own[...]
    di[:, lanes(g1)] = d_own[...]
    pre_out[...] = pre[0:RHS, :]
    beta_out[...] = jnp.broadcast_to(beta, (ROWS, L))[0:RHS, :]
    own_curv = NOISE * jnp.sum(direction * direction, axis=1, keepdims=True)

    recv_wait(6)
    aug_i(1)
    build(1)
    recv_wait(8)

    def image(h, out):
        W = 1024
        for n in range(HALF // W):
            d = slice(n * W, (n + 1) * W)
            out[:, d] = jnp.dot(dj[...], tile[h, :, d], preferred_element_type=F32).astype(out.dtype)

    image(1, im_send)
    send(10, im_send, im_recv, twin)
    expect(10, im_send)
    image(0, im_own)
    recv_wait(9)
    recv_wait(10)
    curv = zero
    for g in range(G):
        d = slice(g * L, (g + 1) * L)
        v = im_own[:, d] + im_recv[:, d].astype(F32)
        im_own[:, d] = v
        curv = curv + v * di[:, d].astype(F32)
    curv = to_row(jnp.sum(curv, axis=1, keepdims=True) + own_curv)
    curv_in = put(zero, NORM, curv)
    for g in range(G):
        d = slice(g * L, (g + 1) * L)
        e5_send[:, d] = (im_own[:, d] + curv_in).astype(BF)

    def send6(dev, g):
        send(11, e5_send.at[:, lanes(g)], e5.at[g1], dev)

    each(dev1, send6)
    expect(11, e5.at[pl.ds(0, G - 1)])
    e5[g1] = e5_send[:, lanes(g1)]
    recv_wait(11)
    tail = e5[0, 32:ROWS, :].astype(F32)
    for g in range(1, G):
        tail = tail + e5[g, 32:ROWS, :].astype(F32)
    keep = (tid >= NORM - 32) & (tid < NORM - 29)
    c2_send[...] = jnp.sum(jnp.where(keep, tail, 0.0), axis=0, keepdims=True)
    mine = c2.at[core * G + g2]

    def send7(dev, _):
        send(12, c2_send, mine, dev)

    def both(t, _):
        for flip in (1, 0):
            for c in (core, other):
                send7(dev2(t, flip, c)[0], 0)
        return 0

    lax.fori_loop(0, 7, both, 0)
    send7(dev2(7, 1, core)[0], 0)
    send7(dev2(7, 1, other)[0], 0)
    send7(twin, 0)
    expect(12, c2.at[pl.ds(0, 2 * G - 1)])
    c2[core * G + g2] = c2_send[...]
    img_out[...] = (total(e5) + NOISE * d40[...])[0:RHS, :]
    recv_wait(12)
    curv_col = jnp.where(cid < RHS, to_col(jnp.sum(c2[...], axis=0)), 1.0)
    alpha = inner_col / curv_col
    alpha_out[...] = jnp.broadcast_to(alpha, (ROWS, L))[0:RHS, :]
    drain()


def solution(mesh):
    axes = ("row", "col")
    pts = P(None, axes)
    placed = (pts, P(), P(axes, None), P(), pts, pts, pts, P())

    def step(points, inv_scale, basis, shrink, sol, res, prev, rz):
        rank = basis.shape[1]
        out = jax.ShapeDtypeStruct((RHS, L), F32)
        v = pl.BlockSpec(memory_space=pltpu.VMEM)
        pre, beta, alpha, img = pl.pallas_call(
            kernel,
            out_shape=(out,) * 4,
            in_specs=[v, v, pl.BlockSpec(memory_space=pl.ANY), v, v, v, v],
            out_specs=(v,) * 4,
            scratch_shapes=[
                pltpu.VMEM((L, rank), BF),
                pltpu.VMEM((ROWS, L), F32),
                pltpu.VMEM((L, L), BF),
                pltpu.VMEM((L, L), BF),
                pltpu.VMEM((2, 2 * L, HALF), BF),
                pltpu.VMEM((HALF, 2 * L), BF),
                pltpu.VMEM((2, HALF, HALF), BF),
                pltpu.VMEM((ROWS, HALF), BF),
                pltpu.VMEM((ROWS, HALF), BF),
                pltpu.VMEM((ROWS, HALF), BF),
                pltpu.VMEM((G, ROWS, L), BF),
                pltpu.VMEM((ROWS, L), BF),
                pltpu.VMEM((G, ROWS, L), BF),
                pltpu.VMEM((ROWS, L), BF),
                pltpu.VMEM((ROWS, rank), BF),
                pltpu.VMEM((ROWS, L), F32),
                pltpu.VMEM((ROWS, L), BF),
                pltpu.VMEM((ROWS, HALF), BF),
                pltpu.VMEM((ROWS, HALF), BF),
                pltpu.VMEM((ROWS, HALF), BF),
                pltpu.VMEM((ROWS, HALF), BF),
                pltpu.VMEM((ROWS, HALF), F32),
                pltpu.VMEM((ROWS, HALF), BF),
                pltpu.VMEM((G, ROWS, L), BF),
                pltpu.VMEM((1, L), F32),
                pltpu.VMEM((2 * G, 1, L), F32),
                pltpu.SemaphoreType.DMA,
                pltpu.SemaphoreType.DMA((15,)),
                pltpu.SemaphoreType.DMA((15,)),
            ],
            compiler_params=pltpu.CompilerParams(
                collective_id=0, has_side_effects=True, vmem_limit_bytes=62 * 1024 * 1024
            ),
            name="cg_step",
        )(
            points, inv_scale.reshape(1, L), basis, shrink.reshape(rank // L, L),
            res, prev, rz.reshape(1, RHS),
        )
        direction = pre + beta * prev
        return sol + alpha * direction, res - alpha * img, direction

    return jax.shard_map(
        step, mesh=mesh, in_specs=placed, out_specs=(pts, pts, pts), check_vma=False
    )
```

```python
import jax
import jax.numpy as jnp
from jax import lax
from jax.experimental import pallas as pl
from jax.experimental.pallas import tpu as pltpu
from jax.sharding import PartitionSpec as P

MESH = pl.DeviceIdType.MESH
BF = jnp.bfloat16
F32 = jnp.float32
NOISE = 0.25
G = 16
L = 128
HALF = G * L
PART = HALF // 2
RHS = 33
ROWS = 40
NORM = 33
INNER = 36


def split3(v):
    hi = v.astype(BF).astype(F32)
    mid = (v - hi).astype(BF).astype(F32)
    return hi, mid, v - hi - mid


def kernel(
    points, inv_scale, basis_hbm, shrink, res, prev, rz,
    pre_out, beta_out, alpha_out, img_out,
    basis, r40, s_own, st_own, si, sj, tile,
    p_send, p_recv, p_half, e1, e2_send, e2, corr_own, corr, d40, d_own, dj, di,
    im_send, im_recv, im_own, e5_send, e5, c2_send, c2,
    basis_sem, ssem, rsem,
):
    row = lax.axis_index("row")
    col = lax.axis_index("col")
    core = row % 2
    y = row // 2
    z = col // 4
    x = col % 4
    xa = x // 2
    xb = ((x + 1) // 2) % 2
    g1 = xb * 8 + z
    g2 = y * 2 + xa
    other = 1 - core
    twin = (y * 2 + other, col)

    def far(t):
        return (4 + ((t + 1) // 2) * (1 - 2 * (t % 2))) % 8

    def dev1(t, flip):
        zz = (z + far(t)) % 8
        b = (xb + flip) % 2
        return (row, zz * 4 + 3 * xa + b - 2 * xa * b), b * 8 + zz

    def dev2(t, flip, c=core):
        yy = (y + far(t)) % 8
        a = (xa + flip) % 2
        return (yy * 2 + c, z * 4 + 3 * a + xb - 2 * a * xb), flip * 8 + t

    def ordered(u, v):
        def dev(t, flip):
            zz = (z + far(t) * u) % 8
            yy = (y + far(t) * v) % 8
            b = (xb + flip * u) % 2
            a = (xa + flip * v) % 2
            place = (yy * 2 + core, zz * 4 + 3 * a + b - 2 * a * b)
            return place, (b * 8 + zz) * u + (a * 8 + yy) * v

        return dev, (xb * 8 + z) * u + (xa * 8 + y) * v

    dev_a, g_a = ordered(other, core)
    dev_b, g_b = ordered(core, other)

    def each(dev, fn, lo=0, hi=8):
        def body(t, _):
            fn(*dev(t, 1))
            fn(*dev(t, 0))
            return 0

        lax.fori_loop(lo, min(hi, 7), body, 0)
        if hi == 8:
            fn(*dev(7, 1))

    def lanes(g):
        return pl.ds(pl.multiple_of(g * L, L), L)

    def send(i, src, dst, dev):
        pltpu.make_async_remote_copy(
            src_ref=src, dst_ref=dst, send_sem=ssem.at[i], recv_sem=rsem.at[i],
            device_id=dev, device_id_type=MESH,
        ).start()

    sent, coming = {}, {}

    def expect(i, ref):
        sent[i] = ref
        coming[i] = ref

    def recv_wait(i):
        ref = coming.pop(i)
        pltpu.make_async_copy(ref, ref, rsem.at[i]).wait()

    def drain():
        for i in list(coming):
            recv_wait(i)
        for i, ref in sent.items():
            pltpu.make_async_copy(ref, ref, ssem.at[i]).wait()

    bar = pltpu.get_barrier_semaphore()
    cp = pltpu.make_async_copy(basis_hbm, basis, basis_sem)
    cp.start()

    def signal(dev, _):
        pl.semaphore_signal(bar, inc=1, device_id=dev, device_id_type=MESH)

    signal(twin, 0)
    each(dev1, signal)
    each(dev2, signal)

    inv_col = jnp.broadcast_to(inv_scale[...], (L, L)).T
    scaled = (points[...].astype(F32) * inv_col).astype(BF)
    s_own[...] = scaled
    st_own[...] = scaled.astype(F32).T.astype(BF)
    si[0, 0:L, lanes(g1)] = s_own[...]
    sj[7 * L : 8 * L, 0:L] = st_own[...]
    for h in range(2):
        si[h, L : 2 * L, :] = jnp.zeros((L, HALF), BF)

    r40[...] = jnp.zeros((ROWS, L), F32)
    r40[0:RHS, :] = res[...]
    r = r40[...]
    r_bf = r.astype(BF)
    rid = lax.broadcasted_iota(jnp.int32, (ROWS, L), 0)
    lid = lax.broadcasted_iota(jnp.int32, (ROWS, L), 1)
    cid = lax.broadcasted_iota(jnp.int32, (ROWS, 1), 0)
    eye = rid == lid

    def to_row(c):
        return jnp.sum(jnp.where(eye, c, 0.0), axis=0, keepdims=True)

    def to_col(v):
        return jnp.sum(jnp.where(eye, v, 0.0), axis=1, keepdims=True)

    def put(v, base, line):
        hi, mid, lo = split3(line)
        v = jnp.where(rid == base, hi, v)
        v = jnp.where(rid == base + 1, mid, v)
        return jnp.where(rid == base + 2, lo, v)

    def take(v, base):
        return jnp.sum(jnp.where((rid >= base) & (rid < base + 3), v, 0.0), axis=0, keepdims=True)

    zero = jnp.zeros((ROWS, L), F32)
    norm = to_row(jnp.sum(r * r, axis=1, keepdims=True))
    norm_in = put(zero, NORM, norm)

    cp.wait()

    def half_of(c):
        return pl.ds(pl.multiple_of(c * HALF, HALF), HALF)

    proj_t = jnp.dot(r_bf, basis[:, half_of(other)], preferred_element_type=F32)
    for g in range(G):
        d = slice(g * L, (g + 1) * L)
        p_send[:, d] = (proj_t[:, d] + norm_in).astype(BF)
    im_own[...] = jnp.dot(r_bf, basis[:, half_of(core)], preferred_element_type=F32)

    pl.semaphore_wait(bar, 2 * (G - 1) + 1)
    send(0, p_send, p_recv, twin)
    expect(0, p_send)

    def send_pts(t, _):
        dev, g = dev2(t, 0)
        send(3, st_own, sj.at[lanes(g), pl.ds(0, L)], dev)
        send(2, s_own, si.at[0, pl.ds(0, L), lanes(g1)], dev1(t, 0)[0])
        return 0

    expect(3, sj.at[pl.ds(0, 7 * L), pl.ds(0, L)])
    expect(2, si.at[0, pl.ds(0, L), pl.ds(0, 7 * L)])
    recv_wait(0)
    norm_in = put(zero, NORM, norm + take(p_recv[:, 0:L].astype(F32), NORM))
    for g in range(G):
        d = slice(g * L, (g + 1) * L)
        v = im_own[:, d] + p_recv[:, d].astype(F32)
        p_half[:, d] = jnp.where(rid < RHS, v, norm_in).astype(BF)

    def send1(dev, g):
        send(1, p_half.at[:, lanes(g)], e1.at[g_a], dev)

    each(dev_a, send1)
    expect(1, e1.at[pl.ds(0, G - 1)])
    lax.fori_loop(0, 3, send_pts, 0)
    e1[g_a] = p_half[:, lanes(g_a)]

    def total(ref):
        acc = ref[0].astype(F32)
        for g in range(1, G):
            acc = acc + ref[g].astype(F32)
        return acc

    recv_wait(1)
    acc = total(e1)
    e2_send[...] = put(acc, NORM, take(acc, NORM)).astype(BF)

    def send2(dev, g):
        send(4, e2_send, e2.at[g_b], dev)

    each(dev_b, send2)
    expect(4, e2.at[pl.ds(0, G - 1)])
    lax.fori_loop(3, 7, send_pts, 0)
    e2[g_b] = e2_send[...]
    recv_wait(4)
    acc = total(e2)
    norm_all = take(acc, NORM)
    proj = jnp.where(rid < RHS, acc, 0.0)
    cor = ((shrink[pl.ds(core * G + g_a, 1), :] - 1.0) * proj).astype(BF).astype(F32)
    inner = to_row(jnp.sum(cor * proj, axis=1, keepdims=True))
    corr_own[...] = put(cor, INNER, inner).astype(BF)

    def send3(dev, g):
        send(5, corr_own, corr.at[:, lanes(core * G + g_a)], dev)

    each(dev_a, send3)
    expect(5, corr.at[:, pl.ds(0, HALF - L)])
    corr[:, lanes(core * G + g_a)] = corr_own[...]

    lane = lax.broadcasted_iota(jnp.int32, (L, L), 1)

    def aug_j(lo, hi):
        def body(n, _):
            v = sj[lanes(n), 0:L].astype(F32)
            hi, mid, lo = split3(jnp.broadcast_to(-0.5 * jnp.sum(v * v, axis=1, keepdims=True), (L, L)))
            ext = jnp.where(lane == 0, hi, jnp.where(lane == 1, mid, jnp.where(lane == 2, lo, 1.0)))
            sj[lanes(n), L : 2 * L] = jnp.where(lane < 6, ext, 0.0).astype(BF)
            return 0

        lax.fori_loop(lo, hi, body, 0)

    def aug_i(h, off):
        W = 512
        line = lax.broadcasted_iota(jnp.int32, (16, W), 0)

        def body(n, _):
            d = pl.ds(pl.multiple_of(off + n * W, W), W)
            v = si[h, 0:L, d].astype(F32)
            hi, mid, lo = split3(-0.5 * jnp.sum(v * v, axis=0, keepdims=True))
            ext = jnp.where(line == 3, hi, jnp.where(line == 4, mid, jnp.where(line == 5, lo, 1.0)))
            si[h, L : L + 16, d] = jnp.where(line < 6, ext, 0.0).astype(BF)
            return 0

        lax.fori_loop(0, PART // W, body, 0)

    def build(h, off, lo, hi):
        W = 512

        def body(k, _):
            e = pl.ds(pl.multiple_of((k // 2) * PART, PART), PART)
            d = pl.ds(pl.multiple_of(off + (k % 2) * W, W), W)
            neg = jnp.dot(sj[e, :], si[h, :, d], preferred_element_type=F32)
            tile[h, e, d] = jnp.exp(jnp.minimum(neg, 0.0)).astype(BF)
            return 0

        lax.fori_loop(2 * lo, 2 * hi, body, 0)

    mine = xb * PART
    rest = (1 - xb) * PART

    def block(h, off):
        return si.at[h, pl.ds(0, L), pl.ds(pl.multiple_of(off, PART), PART)]

    recv_wait(3)
    dst = sj.at[pl.ds(PART, PART), pl.ds(0, L)]
    send(13, sj.at[pl.ds(0, PART), pl.ds(0, L)], dst, dev2(7, 1)[0])
    expect(13, dst)
    recv_wait(2)
    send(14, block(0, mine), block(0, mine), dev1(7, 1)[0])
    expect(14, block(0, mine))
    send(6, block(0, mine), block(1, mine), twin)
    expect(6, block(1, mine))
    aug_j(0, 8)
    aug_i(0, mine)
    build(0, mine, 0, 1)
    recv_wait(5)
    half = corr.at[:, half_of(core)]
    send(7, half, half, twin)
    expect(7, half)

    def apply(c):
        return lax.dot_general(
            corr[:, half_of(c)], basis[:, half_of(c)], (((1,), (1,)), ((), ())),
            preferred_element_type=F32,
        )

    pre = r + apply(core)
    d40[...] = zero
    d40[0:RHS, :] = prev[...]
    rz_row = jnp.concatenate([rz[...], jnp.ones((1, L - RHS), F32)], axis=1)
    rz_col = jnp.where(cid < RHS, to_col(rz_row), 1.0)
    recv_wait(7)
    pre = pre + apply(other)
    tail = corr[32:ROWS, 0:L].astype(F32)
    for g in range(1, 2 * G):
        tail = tail + corr[32:ROWS, g * L : (g + 1) * L].astype(F32)
    tid = lax.broadcasted_iota(jnp.int32, (8, L), 0)
    keep = (tid >= INNER - 32) & (tid < INNER - 29)
    inner = jnp.sum(jnp.where(keep, tail, 0.0), axis=0, keepdims=True)
    inner_col = to_col(inner + norm_all)
    beta = inner_col / rz_col
    direction = jnp.where(rid < RHS, pre + beta * d40[...], 0.0)
    d40[...] = direction
    d_own[...] = direction.astype(BF)

    def send4(dev, g):
        send(8, d_own, dj.at[:, lanes(g)], dev)

    def send5(dev, g):
        send(9, d_own, di.at[:, lanes(g1)], dev)

    each(dev2, send4)
    each(dev1, send5)
    expect(8, dj.at[:, pl.ds(0, HALF - L)])
    expect(9, di.at[:, pl.ds(0, HALF - L)])
    dj[:, 7 * L : 8 * L] = d_own[...]
    di[:, lanes(g1)] = d_own[...]
    pre_out[...] = pre[0:RHS, :]
    beta_out[...] = jnp.broadcast_to(beta, (ROWS, L))[0:RHS, :]
    own_curv = NOISE * jnp.sum(direction * direction, axis=1, keepdims=True)

    recv_wait(14)
    send(15, block(0, rest), block(1, rest), twin)
    expect(15, block(1, rest))
    recv_wait(6)
    aug_i(1, mine)
    build(1, mine, 0, 1)
    recv_wait(13)
    aug_j(8, G)
    build(0, mine, 1, 2)
    build(1, mine, 1, 2)
    aug_i(0, rest)
    build(0, rest, 0, 2)
    recv_wait(15)
    aug_i(1, rest)
    build(1, rest, 0, 2)
    recv_wait(8)

    def image(h, out):
        W = 1024
        for n in range(HALF // W):
            d = slice(n * W, (n + 1) * W)
            out[:, d] = jnp.dot(dj[...], tile[h, :, d], preferred_element_type=F32).astype(out.dtype)

    image(1, im_send)
    send(10, im_send, im_recv, twin)
    expect(10, im_send)
    image(0, im_own)
    recv_wait(9)
    recv_wait(10)
    curv = zero
    for g in range(G):
        d = slice(g * L, (g + 1) * L)
        v = im_own[:, d] + im_recv[:, d].astype(F32)
        im_own[:, d] = v
        curv = curv + v * di[:, d].astype(F32)
    curv = to_row(jnp.sum(curv, axis=1, keepdims=True) + own_curv)
    curv_in = put(zero, NORM, curv)
    for g in range(G):
        d = slice(g * L, (g + 1) * L)
        e5_send[:, d] = (im_own[:, d] + curv_in).astype(BF)

    def send6(dev, g):
        send(11, e5_send.at[:, lanes(g)], e5.at[g1], dev)

    each(dev1, send6)
    expect(11, e5.at[pl.ds(0, G - 1)])
    e5[g1] = e5_send[:, lanes(g1)]
    recv_wait(11)
    tail = e5[0, 32:ROWS, :].astype(F32)
    for g in range(1, G):
        tail = tail + e5[g, 32:ROWS, :].astype(F32)
    keep = (tid >= NORM - 32) & (tid < NORM - 29)
    c2_send[...] = jnp.sum(jnp.where(keep, tail, 0.0), axis=0, keepdims=True)
    slot = c2.at[core * G + g2]

    def send7(dev, _):
        send(12, c2_send, slot, dev)

    def both(t, _):
        for flip in (1, 0):
            for c in (core, other):
                send7(dev2(t, flip, c)[0], 0)
        return 0

    lax.fori_loop(0, 7, both, 0)
    send7(dev2(7, 1, core)[0], 0)
    send7(dev2(7, 1, other)[0], 0)
    send7(twin, 0)
    expect(12, c2.at[pl.ds(0, 2 * G - 1)])
    c2[core * G + g2] = c2_send[...]
    img_out[...] = (total(e5) + NOISE * d40[...])[0:RHS, :]
    recv_wait(12)
    curv_col = jnp.where(cid < RHS, to_col(jnp.sum(c2[...], axis=0)), 1.0)
    alpha = inner_col / curv_col
    alpha_out[...] = jnp.broadcast_to(alpha, (ROWS, L))[0:RHS, :]
    drain()


def solution(mesh):
    axes = ("row", "col")
    pts = P(None, axes)
    placed = (pts, P(), P(axes, None), P(), pts, pts, pts, P())

    def step(points, inv_scale, basis, shrink, sol, res, prev, rz):
        rank = basis.shape[1]
        out = jax.ShapeDtypeStruct((RHS, L), F32)
        v = pl.BlockSpec(memory_space=pltpu.VMEM)
        pre, beta, alpha, img = pl.pallas_call(
            kernel,
            out_shape=(out,) * 4,
            in_specs=[v, v, pl.BlockSpec(memory_space=pl.ANY), v, v, v, v],
            out_specs=(v,) * 4,
            scratch_shapes=[
                pltpu.VMEM((L, rank), BF),
                pltpu.VMEM((ROWS, L), F32),
                pltpu.VMEM((L, L), BF),
                pltpu.VMEM((L, L), BF),
                pltpu.VMEM((2, 2 * L, HALF), BF),
                pltpu.VMEM((HALF, 2 * L), BF),
                pltpu.VMEM((2, HALF, HALF), BF),
                pltpu.VMEM((ROWS, HALF), BF),
                pltpu.VMEM((ROWS, HALF), BF),
                pltpu.VMEM((ROWS, HALF), BF),
                pltpu.VMEM((G, ROWS, L), BF),
                pltpu.VMEM((ROWS, L), BF),
                pltpu.VMEM((G, ROWS, L), BF),
                pltpu.VMEM((ROWS, L), BF),
                pltpu.VMEM((ROWS, rank), BF),
                pltpu.VMEM((ROWS, L), F32),
                pltpu.VMEM((ROWS, L), BF),
                pltpu.VMEM((ROWS, HALF), BF),
                pltpu.VMEM((ROWS, HALF), BF),
                pltpu.VMEM((ROWS, HALF), BF),
                pltpu.VMEM((ROWS, HALF), BF),
                pltpu.VMEM((ROWS, HALF), F32),
                pltpu.VMEM((ROWS, HALF), BF),
                pltpu.VMEM((G, ROWS, L), BF),
                pltpu.VMEM((1, L), F32),
                pltpu.VMEM((2 * G, 1, L), F32),
                pltpu.SemaphoreType.DMA,
                pltpu.SemaphoreType.DMA((16,)),
                pltpu.SemaphoreType.DMA((16,)),
            ],
            compiler_params=pltpu.CompilerParams(
                collective_id=0, has_side_effects=True, vmem_limit_bytes=62 * 1024 * 1024
            ),
            name="cg_step",
        )(
            points, inv_scale.reshape(1, L), basis, shrink.reshape(rank // L, L),
            res, prev, rz.reshape(1, RHS),
        )
        direction = pre + beta * prev
        return sol + alpha * direction, res - alpha * img, direction

    return jax.shard_map(
        step, mesh=mesh, in_specs=placed, out_specs=(pts, pts, pts), check_vma=False
    )
```

```python
import jax
import jax.numpy as jnp
from jax import lax
from jax.experimental import pallas as pl
from jax.experimental.pallas import tpu as pltpu
from jax.sharding import PartitionSpec as P

MESH = pl.DeviceIdType.MESH
BF = jnp.bfloat16
F32 = jnp.float32
NOISE = 0.25
G = 16
L = 128
HALF = G * L
PART = HALF // 2
RHS = 33
ROWS = 40
NORM = 33
INNER = 36


def split3(v):
    hi = v.astype(BF).astype(F32)
    mid = (v - hi).astype(BF).astype(F32)
    return hi, mid, v - hi - mid


def kernel(
    points_h, inv_h, basis_hbm, shrink_h, res_h, prev_h, rz_h,
    pre_out, beta_out, alpha_out, img_out,
    points, inv_scale, shrink, res, prev, rz, basis, r40, s_own, st_own, si, sj, tile,
    p_send, p_recv, p_half, e1, e2_send, e2, corr_own, corr, d40, d_own, dj, di,
    im_send, im_recv, im_own, e5_send, e5, c2_send, c2,
    basis_sem, in_sem, ssem, rsem,
):
    row = lax.axis_index("row")
    col = lax.axis_index("col")
    core = row % 2
    y = row // 2
    z = col // 4
    x = col % 4
    xa = x // 2
    xb = ((x + 1) // 2) % 2
    g1 = xb * 8 + z
    g2 = y * 2 + xa
    other = 1 - core
    twin = (y * 2 + other, col)

    def far(t):
        return (4 + ((t + 1) // 2) * (1 - 2 * (t % 2))) % 8

    def dev1(t, flip):
        zz = (z + far(t)) % 8
        b = (xb + flip) % 2
        return (row, zz * 4 + 3 * xa + b - 2 * xa * b), b * 8 + zz

    def dev2(t, flip, c=core):
        yy = (y + far(t)) % 8
        a = (xa + flip) % 2
        return (yy * 2 + c, z * 4 + 3 * a + xb - 2 * a * xb), flip * 8 + t

    def ordered(u, v):
        def dev(t, flip):
            zz = (z + far(t) * u) % 8
            yy = (y + far(t) * v) % 8
            b = (xb + flip * u) % 2
            a = (xa + flip * v) % 2
            place = (yy * 2 + core, zz * 4 + 3 * a + b - 2 * a * b)
            return place, (b * 8 + zz) * u + (a * 8 + yy) * v

        return dev, (xb * 8 + z) * u + (xa * 8 + y) * v

    dev_a, g_a = ordered(other, core)
    dev_b, g_b = ordered(core, other)

    def each(dev, fn, lo=0, hi=8):
        def body(t, _):
            fn(*dev(t, 1))
            fn(*dev(t, 0))
            return 0

        lax.fori_loop(lo, min(hi, 7), body, 0)
        if hi == 8:
            fn(*dev(7, 1))

    def lanes(g):
        return pl.ds(pl.multiple_of(g * L, L), L)

    def send(i, src, dst, dev):
        pltpu.make_async_remote_copy(
            src_ref=src, dst_ref=dst, send_sem=ssem.at[i], recv_sem=rsem.at[i],
            device_id=dev, device_id_type=MESH,
        ).start()

    sent, coming = {}, {}

    def expect(i, ref):
        sent[i] = ref
        coming[i] = ref

    def recv_wait(i):
        ref = coming.pop(i)
        pltpu.make_async_copy(ref, ref, rsem.at[i]).wait()

    def drain():
        for i in list(coming):
            recv_wait(i)
        for i, ref in sent.items():
            pltpu.make_async_copy(ref, ref, ssem.at[i]).wait()

    bar = pltpu.get_barrier_semaphore()
    cp = pltpu.make_async_copy(basis_hbm, basis, basis_sem)
    ins = [
        pltpu.make_async_copy(a, b, in_sem.at[i])
        for i, (a, b) in enumerate((
            (res_h, res), (points_h, points), (inv_h, inv_scale),
            (shrink_h, shrink), (prev_h, prev), (rz_h, rz),
        ))
    ]
    ins[0].start()
    cp.start()
    for c in ins[1:]:
        c.start()

    def signal(dev, _):
        pl.semaphore_signal(bar, inc=1, device_id=dev, device_id_type=MESH)

    signal(twin, 0)
    each(dev1, signal)
    each(dev2, signal)

    for c in ins:
        c.wait()
    inv_col = jnp.broadcast_to(inv_scale[...], (L, L)).T
    scaled = (points[...].astype(F32) * inv_col).astype(BF)
    s_own[...] = scaled
    st_own[...] = scaled.astype(F32).T.astype(BF)
    si[0, 0:L, lanes(g1)] = s_own[...]
    sj[7 * L : 8 * L, 0:L] = st_own[...]
    for h in range(2):
        si[h, L : 2 * L, :] = jnp.zeros((L, HALF), BF)

    r40[...] = jnp.zeros((ROWS, L), F32)
    r40[0:RHS, :] = res[...]
    r = r40[...]
    r_bf = r.astype(BF)
    rid = lax.broadcasted_iota(jnp.int32, (ROWS, L), 0)
    lid = lax.broadcasted_iota(jnp.int32, (ROWS, L), 1)
    cid = lax.broadcasted_iota(jnp.int32, (ROWS, 1), 0)
    eye = rid == lid

    def to_row(c):
        return jnp.sum(jnp.where(eye, c, 0.0), axis=0, keepdims=True)

    def to_col(v):
        return jnp.sum(jnp.where(eye, v, 0.0), axis=1, keepdims=True)

    def put(v, base, line):
        hi, mid, lo = split3(line)
        v = jnp.where(rid == base, hi, v)
        v = jnp.where(rid == base + 1, mid, v)
        return jnp.where(rid == base + 2, lo, v)

    def take(v, base):
        return jnp.sum(jnp.where((rid >= base) & (rid < base + 3), v, 0.0), axis=0, keepdims=True)

    zero = jnp.zeros((ROWS, L), F32)
    norm = to_row(jnp.sum(r * r, axis=1, keepdims=True))
    norm_in = put(zero, NORM, norm)

    cp.wait()

    def half_of(c):
        return pl.ds(pl.multiple_of(c * HALF, HALF), HALF)

    proj_t = jnp.dot(r_bf, basis[:, half_of(other)], preferred_element_type=F32)
    for g in range(G):
        d = slice(g * L, (g + 1) * L)
        p_send[:, d] = (proj_t[:, d] + norm_in).astype(BF)
    im_own[...] = jnp.dot(r_bf, basis[:, half_of(core)], preferred_element_type=F32)

    pl.semaphore_wait(bar, 2 * (G - 1) + 1)
    send(0, p_send, p_recv, twin)
    expect(0, p_send)

    def send_pts(t, _):
        dev, g = dev2(t, 0)
        send(3, st_own, sj.at[lanes(g), pl.ds(0, L)], dev)
        send(2, s_own, si.at[0, pl.ds(0, L), lanes(g1)], dev1(t, 0)[0])
        return 0

    expect(3, sj.at[pl.ds(0, 7 * L), pl.ds(0, L)])
    expect(2, si.at[0, pl.ds(0, L), pl.ds(0, 7 * L)])
    recv_wait(0)
    norm_in = put(zero, NORM, norm + take(p_recv[:, 0:L].astype(F32), NORM))
    for g in range(G):
        d = slice(g * L, (g + 1) * L)
        v = im_own[:, d] + p_recv[:, d].astype(F32)
        p_half[:, d] = jnp.where(rid < RHS, v, norm_in).astype(BF)

    def send1(dev, g):
        send(1, p_half.at[:, lanes(g)], e1.at[g_a], dev)

    each(dev_a, send1)
    expect(1, e1.at[pl.ds(0, G - 1)])
    lax.fori_loop(0, 7, send_pts, 0)
    e1[g_a] = p_half[:, lanes(g_a)]

    def total(ref):
        acc = ref[0].astype(F32)
        for g in range(1, G):
            acc = acc + ref[g].astype(F32)
        return acc

    recv_wait(1)
    acc = total(e1)
    e2_send[...] = put(acc, NORM, take(acc, NORM)).astype(BF)

    def send2(dev, g):
        send(4, e2_send, e2.at[g_b], dev)

    each(dev_b, send2)
    expect(4, e2.at[pl.ds(0, G - 1)])
    e2[g_b] = e2_send[...]
    mine = xb * PART
    rest = (1 - xb) * PART

    def block(h, off):
        return si.at[h, pl.ds(0, L), pl.ds(pl.multiple_of(off, PART), PART)]

    recv_wait(3)
    dst = sj.at[pl.ds(PART, PART), pl.ds(0, L)]
    send(13, sj.at[pl.ds(0, PART), pl.ds(0, L)], dst, dev2(7, 1)[0])
    expect(13, dst)
    recv_wait(2)
    send(14, block(0, mine), block(0, mine), dev1(7, 1)[0])
    expect(14, block(0, mine))
    send(6, block(0, mine), block(1, mine), twin)
    expect(6, block(1, mine))
    recv_wait(4)
    acc = total(e2)
    norm_all = take(acc, NORM)
    proj = jnp.where(rid < RHS, acc, 0.0)
    cor = ((shrink[pl.ds(core * G + g_a, 1), :] - 1.0) * proj).astype(BF).astype(F32)
    inner = to_row(jnp.sum(cor * proj, axis=1, keepdims=True))
    corr_own[...] = put(cor, INNER, inner).astype(BF)

    def send3(dev, g):
        send(5, corr_own, corr.at[:, lanes(core * G + g_a)], dev)

    each(dev_a, send3)
    expect(5, corr.at[:, pl.ds(0, HALF - L)])
    corr[:, lanes(core * G + g_a)] = corr_own[...]

    lane = lax.broadcasted_iota(jnp.int32, (L, L), 1)

    def aug_j(lo, hi):
        def body(n, _):
            v = sj[lanes(n), 0:L].astype(F32)
            hi, mid, lo = split3(jnp.broadcast_to(-0.5 * jnp.sum(v * v, axis=1, keepdims=True), (L, L)))
            ext = jnp.where(lane == 0, hi, jnp.where(lane == 1, mid, jnp.where(lane == 2, lo, 1.0)))
            sj[lanes(n), L : 2 * L] = jnp.where(lane < 6, ext, 0.0).astype(BF)
            return 0

        lax.fori_loop(lo, hi, body, 0)

    def aug_i(h, off):
        W = 512
        line = lax.broadcasted_iota(jnp.int32, (16, W), 0)

        def body(n, _):
            d = pl.ds(pl.multiple_of(off + n * W, W), W)
            v = si[h, 0:L, d].astype(F32)
            hi, mid, lo = split3(-0.5 * jnp.sum(v * v, axis=0, keepdims=True))
            ext = jnp.where(line == 3, hi, jnp.where(line == 4, mid, jnp.where(line == 5, lo, 1.0)))
            si[h, L : L + 16, d] = jnp.where(line < 6, ext, 0.0).astype(BF)
            return 0

        lax.fori_loop(0, PART // W, body, 0)

    def build(h, off, lo, hi):
        W = 512

        def body(k, _):
            e = pl.ds(pl.multiple_of((k // 2) * PART, PART), PART)
            d = pl.ds(pl.multiple_of(off + (k % 2) * W, W), W)
            neg = jnp.dot(sj[e, :], si[h, :, d], preferred_element_type=F32)
            tile[h, e, d] = jnp.exp(jnp.minimum(neg, 0.0)).astype(BF)
            return 0

        lax.fori_loop(2 * lo, 2 * hi, body, 0)

    aug_j(0, 8)
    aug_i(0, mine)
    build(0, mine, 0, 1)
    recv_wait(6)
    aug_i(1, mine)
    build(1, mine, 0, 1)
    recv_wait(5)
    half = corr.at[:, half_of(core)]
    send(7, half, half, twin)
    expect(7, half)

    def apply(c):
        return lax.dot_general(
            corr[:, half_of(c)], basis[:, half_of(c)], (((1,), (1,)), ((), ())),
            preferred_element_type=F32,
        )

    pre = r + apply(core)
    d40[...] = zero
    d40[0:RHS, :] = prev[...]
    rz_row = jnp.concatenate([rz[...], jnp.ones((1, L - RHS), F32)], axis=1)
    rz_col = jnp.where(cid < RHS, to_col(rz_row), 1.0)
    recv_wait(7)
    pre = pre + apply(other)
    tail = corr[32:ROWS, 0:L].astype(F32)
    for g in range(1, 2 * G):
        tail = tail + corr[32:ROWS, g * L : (g + 1) * L].astype(F32)
    tid = lax.broadcasted_iota(jnp.int32, (8, L), 0)
    keep = (tid >= INNER - 32) & (tid < INNER - 29)
    inner = jnp.sum(jnp.where(keep, tail, 0.0), axis=0, keepdims=True)
    inner_col = to_col(inner + norm_all)
    beta = inner_col / rz_col
    direction = jnp.where(rid < RHS, pre + beta * d40[...], 0.0)
    d40[...] = direction
    d_own[...] = direction.astype(BF)

    def send4(dev, g):
        send(8, d_own, dj.at[:, lanes(g)], dev)

    def send5(dev, g):
        send(9, d_own, di.at[:, lanes(g1)], dev)

    each(dev2, send4)
    each(dev1, send5)
    expect(8, dj.at[:, pl.ds(0, HALF - L)])
    expect(9, di.at[:, pl.ds(0, HALF - L)])
    dj[:, 7 * L : 8 * L] = d_own[...]
    di[:, lanes(g1)] = d_own[...]
    pre_out[...] = pre[0:RHS, :]
    beta_out[...] = jnp.broadcast_to(beta, (ROWS, L))[0:RHS, :]
    own_curv = NOISE * jnp.sum(direction * direction, axis=1, keepdims=True)

    recv_wait(14)
    send(15, block(0, rest), block(1, rest), twin)
    expect(15, block(1, rest))
    recv_wait(13)
    aug_j(8, G)
    build(0, mine, 1, 2)
    build(1, mine, 1, 2)
    aug_i(0, rest)
    build(0, rest, 0, 2)
    recv_wait(15)
    aug_i(1, rest)
    build(1, rest, 0, 2)
    recv_wait(8)

    def image(h, out):
        W = 1024
        for n in range(HALF // W):
            d = slice(n * W, (n + 1) * W)
            out[:, d] = jnp.dot(dj[...], tile[h, :, d], preferred_element_type=F32).astype(out.dtype)

    image(1, im_send)
    send(10, im_send, im_recv, twin)
    expect(10, im_send)
    image(0, im_own)
    recv_wait(9)
    recv_wait(10)
    curv = zero
    for g in range(G):
        d = slice(g * L, (g + 1) * L)
        v = im_own[:, d] + im_recv[:, d].astype(F32)
        im_own[:, d] = v
        curv = curv + v * di[:, d].astype(F32)
    curv = to_row(jnp.sum(curv, axis=1, keepdims=True) + own_curv)
    curv_in = put(zero, NORM, curv)
    for g in range(G):
        d = slice(g * L, (g + 1) * L)
        e5_send[:, d] = (im_own[:, d] + curv_in).astype(BF)

    def send6(dev, g):
        send(11, e5_send.at[:, lanes(g)], e5.at[g1], dev)

    each(dev1, send6)
    expect(11, e5.at[pl.ds(0, G - 1)])
    e5[g1] = e5_send[:, lanes(g1)]
    recv_wait(11)
    tail = e5[0, 32:ROWS, :].astype(F32)
    for g in range(1, G):
        tail = tail + e5[g, 32:ROWS, :].astype(F32)
    keep = (tid >= NORM - 32) & (tid < NORM - 29)
    c2_send[...] = jnp.sum(jnp.where(keep, tail, 0.0), axis=0, keepdims=True)
    slot = c2.at[core * G + g2]

    def send7(dev, _):
        send(12, c2_send, slot, dev)

    def both(t, _):
        for flip in (1, 0):
            for c in (core, other):
                send7(dev2(t, flip, c)[0], 0)
        return 0

    lax.fori_loop(0, 7, both, 0)
    send7(dev2(7, 1, core)[0], 0)
    send7(dev2(7, 1, other)[0], 0)
    send7(twin, 0)
    expect(12, c2.at[pl.ds(0, 2 * G - 1)])
    c2[core * G + g2] = c2_send[...]
    img_out[...] = (total(e5) + NOISE * d40[...])[0:RHS, :]
    recv_wait(12)
    curv_col = jnp.where(cid < RHS, to_col(jnp.sum(c2[...], axis=0)), 1.0)
    alpha = inner_col / curv_col
    alpha_out[...] = jnp.broadcast_to(alpha, (ROWS, L))[0:RHS, :]
    drain()


def solution(mesh):
    axes = ("row", "col")
    pts = P(None, axes)
    placed = (pts, P(), P(axes, None), P(), pts, pts, pts, P())

    def step(points, inv_scale, basis, shrink, sol, res, prev, rz):
        rank = basis.shape[1]
        out = jax.ShapeDtypeStruct((RHS, L), F32)
        v = pl.BlockSpec(memory_space=pltpu.VMEM)
        pre, beta, alpha, img = pl.pallas_call(
            kernel,
            out_shape=(out,) * 4,
            in_specs=[pl.BlockSpec(memory_space=pl.ANY)] * 7,
            out_specs=(v,) * 4,
            scratch_shapes=[
                pltpu.VMEM((L, L), BF),
                pltpu.VMEM((1, L), F32),
                pltpu.VMEM((rank // L, L), F32),
                pltpu.VMEM((RHS, L), F32),
                pltpu.VMEM((RHS, L), F32),
                pltpu.VMEM((1, RHS), F32),
                pltpu.VMEM((L, rank), BF),
                pltpu.VMEM((ROWS, L), F32),
                pltpu.VMEM((L, L), BF),
                pltpu.VMEM((L, L), BF),
                pltpu.VMEM((2, 2 * L, HALF), BF),
                pltpu.VMEM((HALF, 2 * L), BF),
                pltpu.VMEM((2, HALF, HALF), BF),
                pltpu.VMEM((ROWS, HALF), BF),
                pltpu.VMEM((ROWS, HALF), BF),
                pltpu.VMEM((ROWS, HALF), BF),
                pltpu.VMEM((G, ROWS, L), BF),
                pltpu.VMEM((ROWS, L), BF),
                pltpu.VMEM((G, ROWS, L), BF),
                pltpu.VMEM((ROWS, L), BF),
                pltpu.VMEM((ROWS, rank), BF),
                pltpu.VMEM((ROWS, L), F32),
                pltpu.VMEM((ROWS, L), BF),
                pltpu.VMEM((ROWS, HALF), BF),
                pltpu.VMEM((ROWS, HALF), BF),
                pltpu.VMEM((ROWS, HALF), BF),
                pltpu.VMEM((ROWS, HALF), BF),
                pltpu.VMEM((ROWS, HALF), F32),
                pltpu.VMEM((ROWS, HALF), BF),
                pltpu.VMEM((G, ROWS, L), BF),
                pltpu.VMEM((1, L), F32),
                pltpu.VMEM((2 * G, 1, L), F32),
                pltpu.SemaphoreType.DMA,
                pltpu.SemaphoreType.DMA((6,)),
                pltpu.SemaphoreType.DMA((16,)),
                pltpu.SemaphoreType.DMA((16,)),
            ],
            compiler_params=pltpu.CompilerParams(
                collective_id=0, has_side_effects=True, vmem_limit_bytes=62 * 1024 * 1024
            ),
            name="cg_step",
        )(
            points, inv_scale.reshape(1, L), basis, shrink.reshape(rank // L, L),
            res, prev, rz.reshape(1, RHS),
        )
        direction = pre + beta * prev
        return sol + alpha * direction, res - alpha * img, direction

    return jax.shard_map(
        step, mesh=mesh, in_specs=placed, out_specs=(pts, pts, pts), check_vma=False
    )
```

```python
import jax
import jax.numpy as jnp
from jax import lax
from jax.experimental import pallas as pl
from jax.experimental.pallas import tpu as pltpu
from jax.sharding import PartitionSpec as P

MESH = pl.DeviceIdType.MESH
BF = jnp.bfloat16
F32 = jnp.float32
NOISE = 0.25
G = 16
L = 128
HALF = G * L
PART = HALF // 2
RHS = 33
ROWS = 40
NORM = 33
INNER = 36


def split3(v):
    hi = v.astype(BF).astype(F32)
    mid = (v - hi).astype(BF).astype(F32)
    return hi, mid, v - hi - mid


def kernel(
    points_h, inv_h, basis_hbm, shrink_h, res_h, prev_h, rz_h,
    pre_out, beta_out, alpha_out, img_out,
    points, inv_scale, shrink, res, prev, rz, basis, r40, s_own, st_own, si, sj, tile,
    p_send, p_recv, p_half, e1, e2_send, e2, corr_own, corr, d40, d_own, dj, di,
    im_send, im_recv, im_own, e5_send, e5, c2_send, c2,
    basis_sem, in_sem, ssem, rsem,
):
    row = lax.axis_index("row")
    col = lax.axis_index("col")
    core = row % 2
    y = row // 2
    z = col // 4
    x = col % 4
    xa = x // 2
    xb = ((x + 1) // 2) % 2
    g1 = xb * 8 + z
    g2 = y * 2 + xa
    other = 1 - core
    twin = (y * 2 + other, col)

    def far(t):
        return (4 + ((t + 1) // 2) * (1 - 2 * (t % 2))) % 8

    def dev1(t, flip):
        zz = (z + far(t)) % 8
        b = (xb + flip) % 2
        return (row, zz * 4 + 3 * xa + b - 2 * xa * b), b * 8 + zz

    def dev2(t, flip, c=core):
        yy = (y + far(t)) % 8
        a = (xa + flip) % 2
        return (yy * 2 + c, z * 4 + 3 * a + xb - 2 * a * xb), flip * 8 + t

    def ordered(u, v):
        def dev(t, flip):
            zz = (z + far(t) * u) % 8
            yy = (y + far(t) * v) % 8
            b = (xb + flip * u) % 2
            a = (xa + flip * v) % 2
            place = (yy * 2 + core, zz * 4 + 3 * a + b - 2 * a * b)
            return place, (b * 8 + zz) * u + (a * 8 + yy) * v

        return dev, (xb * 8 + z) * u + (xa * 8 + y) * v

    dev_a, g_a = ordered(other, core)
    dev_b, g_b = ordered(core, other)

    def each(dev, fn, lo=0, hi=8):
        def body(t, _):
            fn(*dev(t, 1))
            fn(*dev(t, 0))
            return 0

        lax.fori_loop(lo, min(hi, 7), body, 0)
        if hi == 8:
            fn(*dev(7, 1))

    def lanes(g):
        return pl.ds(pl.multiple_of(g * L, L), L)

    def send(i, src, dst, dev):
        pltpu.make_async_remote_copy(
            src_ref=src, dst_ref=dst, send_sem=ssem.at[i], recv_sem=rsem.at[i],
            device_id=dev, device_id_type=MESH,
        ).start()

    sent, coming = {}, {}

    def expect(i, ref):
        sent[i] = ref
        coming[i] = ref

    def recv_wait(i):
        ref = coming.pop(i)
        pltpu.make_async_copy(ref, ref, rsem.at[i]).wait()

    def drain():
        for i in list(coming):
            recv_wait(i)
        for i, ref in sent.items():
            pltpu.make_async_copy(ref, ref, ssem.at[i]).wait()

    bar = pltpu.get_barrier_semaphore()
    cp = pltpu.make_async_copy(basis_hbm, basis, basis_sem)
    ins = [
        pltpu.make_async_copy(a, b, in_sem.at[i])
        for i, (a, b) in enumerate((
            (res_h, res), (points_h, points), (inv_h, inv_scale),
            (shrink_h, shrink), (prev_h, prev), (rz_h, rz),
        ))
    ]
    ins[0].start()
    cp.start()
    for c in ins[1:]:
        c.start()

    def signal(dev, _):
        pl.semaphore_signal(bar, inc=1, device_id=dev, device_id_type=MESH)

    signal(twin, 0)
    each(dev1, signal)
    each(dev2, signal)

    for c in ins:
        c.wait()
    inv_col = jnp.broadcast_to(inv_scale[...], (L, L)).T
    scaled = (points[...].astype(F32) * inv_col).astype(BF)
    s_own[...] = scaled
    st_own[...] = scaled.astype(F32).T.astype(BF)
    si[0, 0:L, lanes(g1)] = s_own[...]
    sj[7 * L : 8 * L, 0:L] = st_own[...]
    for h in range(2):
        si[h, L : 2 * L, :] = jnp.zeros((L, HALF), BF)

    r40[...] = jnp.zeros((ROWS, L), F32)
    r40[0:RHS, :] = res[...]
    r = r40[...]
    r_bf = r.astype(BF)
    rid = lax.broadcasted_iota(jnp.int32, (ROWS, L), 0)
    lid = lax.broadcasted_iota(jnp.int32, (ROWS, L), 1)
    cid = lax.broadcasted_iota(jnp.int32, (ROWS, 1), 0)
    eye = rid == lid

    def to_row(c):
        return jnp.sum(jnp.where(eye, c, 0.0), axis=0, keepdims=True)

    def to_col(v):
        return jnp.sum(jnp.where(eye, v, 0.0), axis=1, keepdims=True)

    def put(v, base, line):
        hi, mid, lo = split3(line)
        v = jnp.where(rid == base, hi, v)
        v = jnp.where(rid == base + 1, mid, v)
        return jnp.where(rid == base + 2, lo, v)

    def take(v, base):
        return jnp.sum(jnp.where((rid >= base) & (rid < base + 3), v, 0.0), axis=0, keepdims=True)

    zero = jnp.zeros((ROWS, L), F32)
    norm = to_row(jnp.sum(r * r, axis=1, keepdims=True))
    norm_in = put(zero, NORM, norm)

    cp.wait()

    def half_of(c):
        return pl.ds(pl.multiple_of(c * HALF, HALF), HALF)

    proj_t = jnp.dot(r_bf, basis[:, half_of(other)], preferred_element_type=F32)
    p_send[:, 0:L] = (proj_t[:, 0:L] + norm_in).astype(BF)
    p_send[:, L:HALF] = proj_t[:, L:HALF].astype(BF)
    im_own[...] = jnp.dot(r_bf, basis[:, half_of(core)], preferred_element_type=F32)

    pl.semaphore_wait(bar, 2 * (G - 1) + 1)
    send(0, p_send, p_recv, twin)
    expect(0, p_send)

    def send_pts(t, _):
        dev, g = dev2(t, 0)
        send(3, st_own, sj.at[lanes(g), pl.ds(0, L)], dev)
        send(2, s_own, si.at[0, pl.ds(0, L), lanes(g1)], dev1(t, 0)[0])
        return 0

    expect(3, sj.at[pl.ds(0, 7 * L), pl.ds(0, L)])
    expect(2, si.at[0, pl.ds(0, L), pl.ds(0, 7 * L)])
    recv_wait(0)
    norm_in = put(zero, NORM, norm + take(p_recv[:, 0:L].astype(F32), NORM))
    for g in range(G):
        d = slice(g * L, (g + 1) * L)
        v = im_own[:, d] + p_recv[:, d].astype(F32)
        p_half[:, d] = jnp.where(rid < RHS, v, norm_in).astype(BF)

    def send1(dev, g):
        send(1, p_half.at[:, lanes(g)], e1.at[g_a], dev)

    each(dev_a, send1)
    expect(1, e1.at[pl.ds(0, G - 1)])
    lax.fori_loop(0, 7, send_pts, 0)
    e1[g_a] = p_half[:, lanes(g_a)]

    def total(ref):
        acc = ref[0].astype(F32)
        for g in range(1, G):
            acc = acc + ref[g].astype(F32)
        return acc

    recv_wait(1)
    acc = total(e1)
    e2_send[...] = put(acc, NORM, take(acc, NORM)).astype(BF)

    def send2(dev, g):
        send(4, e2_send, e2.at[g_b], dev)

    each(dev_b, send2)
    expect(4, e2.at[pl.ds(0, G - 1)])
    e2[g_b] = e2_send[...]
    mine = xb * PART
    rest = (1 - xb) * PART

    def block(h, off):
        return si.at[h, pl.ds(0, L), pl.ds(pl.multiple_of(off, PART), PART)]

    recv_wait(3)
    dst = sj.at[pl.ds(PART, PART), pl.ds(0, L)]
    send(13, sj.at[pl.ds(0, PART), pl.ds(0, L)], dst, dev2(7, 1)[0])
    expect(13, dst)
    recv_wait(2)
    send(14, block(0, mine), block(0, mine), dev1(7, 1)[0])
    expect(14, block(0, mine))
    send(6, block(0, mine), block(1, mine), twin)
    expect(6, block(1, mine))
    lane = lax.broadcasted_iota(jnp.int32, (L, L), 1)

    def aug_j(lo, hi):
        def body(n, _):
            v = sj[lanes(n), 0:L].astype(F32)
            hi, mid, lo = split3(jnp.broadcast_to(-0.5 * jnp.sum(v * v, axis=1, keepdims=True), (L, L)))
            ext = jnp.where(lane == 0, hi, jnp.where(lane == 1, mid, jnp.where(lane == 2, lo, 1.0)))
            sj[lanes(n), L : 2 * L] = jnp.where(lane < 6, ext, 0.0).astype(BF)
            return 0

        lax.fori_loop(lo, hi, body, 0)

    def aug_i(h, off):
        W = 512
        line = lax.broadcasted_iota(jnp.int32, (16, W), 0)

        def body(n, _):
            d = pl.ds(pl.multiple_of(off + n * W, W), W)
            v = si[h, 0:L, d].astype(F32)
            hi, mid, lo = split3(-0.5 * jnp.sum(v * v, axis=0, keepdims=True))
            ext = jnp.where(line == 3, hi, jnp.where(line == 4, mid, jnp.where(line == 5, lo, 1.0)))
            si[h, L : L + 16, d] = jnp.where(line < 6, ext, 0.0).astype(BF)
            return 0

        lax.fori_loop(0, PART // W, body, 0)

    def build(h, off, lo, hi):
        d = pl.ds(pl.multiple_of(off, PART), PART)

        def body(k, _):
            e = pl.ds(pl.multiple_of(k * PART, PART), PART)
            neg = jnp.dot(sj[e, :], si[h, :, d], preferred_element_type=F32)
            tile[h, e, d] = jnp.exp(jnp.minimum(neg, 0.0)).astype(BF)
            return 0

        lax.fori_loop(lo, hi, body, 0)

    aug_j(0, 8)
    aug_i(0, mine)
    recv_wait(4)
    acc = total(e2)
    norm_all = take(acc, NORM)
    proj = jnp.where(rid < RHS, acc, 0.0)
    cor = ((shrink[pl.ds(core * G + g_a, 1), :] - 1.0) * proj).astype(BF).astype(F32)
    inner = to_row(jnp.sum(cor * proj, axis=1, keepdims=True))
    corr_own[...] = put(cor, INNER, inner).astype(BF)

    def send3(dev, g):
        send(5, corr_own, corr.at[:, lanes(core * G + g_a)], dev)

    each(dev_a, send3)
    expect(5, corr.at[:, pl.ds(0, HALF - L)])
    corr[:, lanes(core * G + g_a)] = corr_own[...]

    build(0, mine, 0, 1)
    recv_wait(6)
    aug_i(1, mine)
    build(1, mine, 0, 1)
    recv_wait(5)
    half = corr.at[:, half_of(core)]
    send(7, half, half, twin)
    expect(7, half)

    def apply(c):
        return lax.dot_general(
            corr[:, half_of(c)], basis[:, half_of(c)], (((1,), (1,)), ((), ())),
            preferred_element_type=F32,
        )

    pre = r + apply(core)
    d40[...] = zero
    d40[0:RHS, :] = prev[...]
    rz_row = jnp.concatenate([rz[...], jnp.ones((1, L - RHS), F32)], axis=1)
    rz_col = jnp.where(cid < RHS, to_col(rz_row), 1.0)
    recv_wait(13)
    aug_j(8, G)
    build(0, mine, 1, 2)
    recv_wait(7)
    pre = pre + apply(other)
    tail = corr[32:ROWS, 0:L].astype(F32)
    for g in range(1, 2 * G):
        tail = tail + corr[32:ROWS, g * L : (g + 1) * L].astype(F32)
    tid = lax.broadcasted_iota(jnp.int32, (8, L), 0)
    keep = (tid >= INNER - 32) & (tid < INNER - 29)
    inner = jnp.sum(jnp.where(keep, tail, 0.0), axis=0, keepdims=True)
    inner_col = to_col(inner + norm_all)
    beta = inner_col / rz_col
    direction = jnp.where(rid < RHS, pre + beta * d40[...], 0.0)
    d40[...] = direction
    d_own[...] = direction.astype(BF)

    def send4(dev, g):
        send(8, d_own, dj.at[:, lanes(g)], dev)

    def send5(dev, g):
        send(9, d_own, di.at[:, lanes(g1)], dev)

    each(dev2, send4)
    each(dev1, send5)
    expect(8, dj.at[:, pl.ds(0, HALF - L)])
    expect(9, di.at[:, pl.ds(0, HALF - L)])
    dj[:, 7 * L : 8 * L] = d_own[...]
    di[:, lanes(g1)] = d_own[...]
    pre_out[...] = pre[0:RHS, :]
    beta_out[...] = jnp.broadcast_to(beta, (ROWS, L))[0:RHS, :]
    own_curv = NOISE * jnp.sum(direction * direction, axis=1, keepdims=True)

    recv_wait(14)
    send(15, block(0, rest), block(1, rest), twin)
    expect(15, block(1, rest))
    build(1, mine, 1, 2)
    aug_i(0, rest)
    build(0, rest, 0, 2)
    recv_wait(15)
    aug_i(1, rest)
    build(1, rest, 0, 2)
    recv_wait(8)

    def image(h, out):
        W = 1024
        for n in range(HALF // W):
            d = slice(n * W, (n + 1) * W)
            out[:, d] = jnp.dot(dj[...], tile[h, :, d], preferred_element_type=F32).astype(out.dtype)

    image(1, im_send)
    send(10, im_send, im_recv, twin)
    expect(10, im_send)
    image(0, im_own)
    recv_wait(9)
    recv_wait(10)
    curv = zero
    for g in range(G):
        d = slice(g * L, (g + 1) * L)
        v = im_own[:, d] + im_recv[:, d].astype(F32)
        im_own[:, d] = v
        curv = curv + v * di[:, d].astype(F32)
    curv = to_row(jnp.sum(curv, axis=1, keepdims=True) + own_curv)
    curv_in = put(zero, NORM, curv)
    for g in range(G):
        d = slice(g * L, (g + 1) * L)
        e5_send[:, d] = (im_own[:, d] + curv_in).astype(BF)

    def send6(dev, g):
        send(11, e5_send.at[:, lanes(g)], e5.at[g1], dev)

    each(dev1, send6)
    expect(11, e5.at[pl.ds(0, G - 1)])
    e5[g1] = e5_send[:, lanes(g1)]
    recv_wait(11)
    tail = e5[0, 32:ROWS, :].astype(F32)
    for g in range(1, G):
        tail = tail + e5[g, 32:ROWS, :].astype(F32)
    keep = (tid >= NORM - 32) & (tid < NORM - 29)
    c2_send[...] = jnp.sum(jnp.where(keep, tail, 0.0), axis=0, keepdims=True)
    slot = c2.at[core * G + g2]

    def send7(dev, _):
        send(12, c2_send, slot, dev)

    def both(t, _):
        for flip in (1, 0):
            for c in (core, other):
                send7(dev2(t, flip, c)[0], 0)
        return 0

    lax.fori_loop(0, 7, both, 0)
    send7(dev2(7, 1, core)[0], 0)
    send7(dev2(7, 1, other)[0], 0)
    send7(twin, 0)
    expect(12, c2.at[pl.ds(0, 2 * G - 1)])
    c2[core * G + g2] = c2_send[...]
    img_out[...] = (total(e5) + NOISE * d40[...])[0:RHS, :]
    recv_wait(12)
    curv_col = jnp.where(cid < RHS, to_col(jnp.sum(c2[...], axis=0)), 1.0)
    alpha = inner_col / curv_col
    alpha_out[...] = jnp.broadcast_to(alpha, (ROWS, L))[0:RHS, :]
    drain()


def solution(mesh):
    axes = ("row", "col")
    pts = P(None, axes)
    placed = (pts, P(), P(axes, None), P(), pts, pts, pts, P())

    def step(points, inv_scale, basis, shrink, sol, res, prev, rz):
        rank = basis.shape[1]
        out = jax.ShapeDtypeStruct((RHS, L), F32)
        v = pl.BlockSpec(memory_space=pltpu.VMEM)
        pre, beta, alpha, img = pl.pallas_call(
            kernel,
            out_shape=(out,) * 4,
            in_specs=[pl.BlockSpec(memory_space=pl.ANY)] * 7,
            out_specs=(v,) * 4,
            scratch_shapes=[
                pltpu.VMEM((L, L), BF),
                pltpu.VMEM((1, L), F32),
                pltpu.VMEM((rank // L, L), F32),
                pltpu.VMEM((RHS, L), F32),
                pltpu.VMEM((RHS, L), F32),
                pltpu.VMEM((1, RHS), F32),
                pltpu.VMEM((L, rank), BF),
                pltpu.VMEM((ROWS, L), F32),
                pltpu.VMEM((L, L), BF),
                pltpu.VMEM((L, L), BF),
                pltpu.VMEM((2, 2 * L, HALF), BF),
                pltpu.VMEM((HALF, 2 * L), BF),
                pltpu.VMEM((2, HALF, HALF), BF),
                pltpu.VMEM((ROWS, HALF), BF),
                pltpu.VMEM((ROWS, HALF), BF),
                pltpu.VMEM((ROWS, HALF), BF),
                pltpu.VMEM((G, ROWS, L), BF),
                pltpu.VMEM((ROWS, L), BF),
                pltpu.VMEM((G, ROWS, L), BF),
                pltpu.VMEM((ROWS, L), BF),
                pltpu.VMEM((ROWS, rank), BF),
                pltpu.VMEM((ROWS, L), F32),
                pltpu.VMEM((ROWS, L), BF),
                pltpu.VMEM((ROWS, HALF), BF),
                pltpu.VMEM((ROWS, HALF), BF),
                pltpu.VMEM((ROWS, HALF), BF),
                pltpu.VMEM((ROWS, HALF), BF),
                pltpu.VMEM((ROWS, HALF), F32),
                pltpu.VMEM((ROWS, HALF), BF),
                pltpu.VMEM((G, ROWS, L), BF),
                pltpu.VMEM((1, L), F32),
                pltpu.VMEM((2 * G, 1, L), F32),
                pltpu.SemaphoreType.DMA,
                pltpu.SemaphoreType.DMA((6,)),
                pltpu.SemaphoreType.DMA((16,)),
                pltpu.SemaphoreType.DMA((16,)),
            ],
            compiler_params=pltpu.CompilerParams(
                collective_id=0, has_side_effects=True, vmem_limit_bytes=62 * 1024 * 1024
            ),
            name="cg_step",
        )(
            points, inv_scale.reshape(1, L), basis, shrink.reshape(rank // L, L),
            res, prev, rz.reshape(1, RHS),
        )
        direction = pre + beta * prev
        return sol + alpha * direction, res - alpha * img, direction

    return jax.shard_map(
        step, mesh=mesh, in_specs=placed, out_specs=(pts, pts, pts), check_vma=False
    )
```
